512 devices in a mesh: region: 32 (over z, core), client: 16 (over x, y).
Axes of the slice: x: 4, y: 4, z: 16, core: 2. Of those that a mesh axis runs over, the one named last changes fastest.
Arguments:
- private_design: bfloat16 [32, 16, 512, 512], P('region', 'client'), may hold values from -0.25 to 0.25
- regional_design: bfloat16 [32, 16, 512, 512], P('region', 'client'), may hold values from -0.0625 to 0.0625
- global_design: bfloat16 [32, 16, 512, 256], P('region', 'client'), may hold values from -0.01171875 to 0.01171875
- targets: bfloat16 [32, 16, 512, 256], P('region', 'client'), may hold values from -6 to 6
- private_prior: float32 [32, 16, 512], P('region', 'client'), may hold values from 0.25 to 2
- regional_prior: float32 [32, 512], P('region'), may hold values from 0.25 to 2
- global_prior: float32 [256], replicated, may hold values from 0.25 to 2
Outputs:
- private_solution: float32 [32, 16, 512, 256], P('region', 'client')
- regional_solution: float32 [32, 512, 256], P('region', 'client')
- global_solution: float32 [256, 256], P('region')
The draws below stay inside these ranges and needn't reach their ends.
All inputs are finite; a program needn't handle non-finite values.
Results may differ from the reference program's by a relative error of at most 0.0003.
Values sent between devices are 32-bit elements; how exact they have to be, the bound alone decides.
A program may use at most 64 MiB of HBM per device.

```python
import math
import jax
import jax.numpy as jnp
from jax import lax

P_SIZE = 512
R = 512
G = 256
NRHS = 256
ROWS = 512
CLIENTS = 16
REGIONS = 32


def levels(stream_key, dims, pieces, smallest, high):
    level = 1.0
    for dim, blocks in pieces:
        steps = jax.random.uniform(jax.random.fold_in(jax.random.fold_in(stream_key, 6), dim), (blocks,), jnp.float32, smallest / len(pieces), high / len(pieces))
        level = level * jnp.repeat(jnp.exp(steps), dims[dim] // blocks).reshape((-1,) + (1,) * (len(dims) - 1 - dim))
    return level


def gaussian(own_key, shape, spread, reach, pieces=(), kind=jnp.bfloat16):
    result = spread * jax.random.normal(own_key, shape, jnp.float32)
    if pieces:
        result = result * levels(own_key, shape, pieces, -0.22, 0.18)
    return jnp.clip(result, -reach, reach).astype(kind)


def setup_inputs(seed: int = 0) -> dict:
    seeds = jax.random.split(jax.random.key(seed), 8)
    return {
        "private_design": gaussian(seeds[0], (REGIONS, CLIENTS, ROWS, P_SIZE), ROWS ** -0.5, 0.25, ((0, 32), (1, 16))),
        "regional_design": gaussian(seeds[1], (REGIONS, CLIENTS, ROWS, R), (ROWS * CLIENTS) ** -0.5, 0.0625, ((0, 32), (1, 16))),
        "global_design": gaussian(seeds[2], (REGIONS, CLIENTS, ROWS, G), (ROWS * CLIENTS * REGIONS) ** -0.5, 0.01171875, ((0, 32), (1, 16))),
        "targets": gaussian(seeds[3], (REGIONS, CLIENTS, ROWS, NRHS), 1.0, 6.0, ((0, 32), (1, 16))),
        "private_prior": jnp.clip(jnp.exp(math.log(2.0) - 2.0794415 * jax.random.uniform(seeds[4], (REGIONS, CLIENTS, P_SIZE), jnp.float32) ** levels(seeds[4], (REGIONS, CLIENTS, P_SIZE), ((0, 32), (1, 16)), -0.2, 0.2)), 0.25, 2.0),
        "regional_prior": jnp.clip(jnp.exp(math.log(2.0) - 2.0794415 * jax.random.uniform(seeds[5], (REGIONS, R), jnp.float32) ** levels(seeds[5], (REGIONS, R), ((0, 32),), -0.2, 0.2)), 0.25, 2.0),
        "global_prior": jnp.clip(jnp.exp(jax.random.uniform(seeds[6], (G,), jnp.float32, math.log(0.25), math.log(2.0))), 0.25, 2.0),
    }


def lower_solve(factor, rhs, transpose):
    return lax.linalg.triangular_solve(factor, rhs, left_side=True, lower=True, transpose_a=transpose)

def inner(left, right):
    return lax.dot_general(left.astype(jnp.float32), right.astype(jnp.float32), (((0,), (0,)), ((), ())), preferred_element_type=jnp.float32, precision=lax.Precision.HIGHEST)

def matmul(left, right):
    return jnp.dot(left.astype(jnp.float32), right.astype(jnp.float32), preferred_element_type=jnp.float32, precision=lax.Precision.HIGHEST)

def client_part(design, side, data, prior):
    joined = jnp.concatenate([side, data], axis=1)
    gram = inner(design, design) + jnp.diag(prior)
    coupling = inner(design, joined)
    side_gram = inner(side, joined)
    factor = jnp.linalg.cholesky(gram)
    solved = lower_solve(factor, coupling, False)
    contrib = side_gram - inner(solved[:, :R + G], solved)
    return (contrib, factor, solved)

def region_part(items):
    design, regional, globe, data, prior, reg_prior = items
    side = jnp.concatenate([regional, globe], axis=2)
    contribs, factors, solveds = lax.map(lambda one: client_part(*one), (design, side, data, prior))
    summed = jnp.sum(contribs, axis=0)
    block = summed[:R, :R] + jnp.diag(reg_prior)
    reg_factor = jnp.linalg.cholesky(block)
    reg_solved = lower_solve(reg_factor, summed[:R, R:], False)
    global_term = summed[R:, R:] - inner(reg_solved[:, :G], reg_solved)
    return (global_term, factors, solveds, reg_factor, reg_solved)

def reference(private_design, regional_design, global_design, targets, private_prior, regional_prior, global_prior):
    terms, factors, solveds, reg_factors, reg_solveds = lax.map(region_part, (private_design, regional_design, global_design, targets, private_prior, regional_prior))
    total = jnp.sum(terms, axis=0)
    hessian = total[:, :G] + jnp.diag(global_prior)
    glob_factor = jnp.linalg.cholesky(hessian)
    global_solution = lower_solve(glob_factor, lower_solve(glob_factor, total[:, G:], False), True)

    def region_back(items):
        reg_factor, reg_solved, factor_set, solved_set = items
        regional = lower_solve(reg_factor, reg_solved[:, G:] - matmul(reg_solved[:, :G], global_solution), True)
        stacked = jnp.concatenate([regional, global_solution], axis=0)

        def client_back(pair):
            factor, solved = pair
            return lower_solve(factor, solved[:, R + G:] - matmul(solved[:, :R + G], stacked), True)
        return (lax.map(client_back, (factor_set, solved_set)), regional)
    private_solution, regional_solution = lax.map(region_back, (reg_factors, reg_solveds, factors, solveds))
    return (private_solution, regional_solution, global_solution)
```

```python
import functools

import jax
import jax.numpy as jnp
from jax import lax
from jax.experimental import pallas as pl
from jax.experimental.pallas import tpu as pltpu
from jax.sharding import PartitionSpec as P

F32 = jnp.float32
BF16 = jnp.bfloat16
MESH = pl.DeviceIdType.MESH
HIGHEST = lax.Precision.HIGHEST
LEAF = 128
SIDE = 4
VMEM = pl.BlockSpec(memory_space=pltpu.VMEM)


def split(x):
    high = x.astype(BF16)
    return high, (x - high.astype(F32)).astype(BF16)


def mm(a, b):
    return jnp.dot(a, b, preferred_element_type=F32)


def mm3(a, b):
    a_high, a_low = split(a)
    b_high, b_low = split(b)
    return mm(a_high, b_high) + (mm(a_high, b_low) + mm(a_low, b_high))


def mm_full(a, b):
    return jnp.dot(a, b, preferred_element_type=F32, precision=HIGHEST)


def tree(terms):
    while len(terms) > 1:
        terms = [
            terms[i] + terms[i + 1] if i + 1 < len(terms) else terms[i]
            for i in range(0, len(terms), 2)
        ]
    return terms[0]


def reciprocal(d):
    r = pltpu.reciprocal(d, approx=True)
    return r * (2.0 - d * r)


def leaf_inverse(m_ref):
    n = LEAF
    strips = n // 8
    lane = lax.broadcasted_iota(jnp.int32, (8, n), 1)
    sub = lax.broadcasted_iota(jnp.int32, (8, n), 0)
    is_row = [sub == k for k in range(8)]

    def row(v, k):
        return jnp.broadcast_to(v[k : k + 1, :], (8, n))

    def column(v, l):
        return jnp.broadcast_to(v[:, l : l + 1], (8, n))

    strip = [m_ref[8 * i : 8 * i + 8, :] for i in range(strips)]
    for k in range(strips):
        first = 8 * k
        cols = [column(strip[k], first + c) for c in range(8)]
        inside = (lane >= first) & (lane < first + 8)
        out = jnp.where(inside, jnp.where(lane - first == sub, 1.0, 0.0), strip[k])
        pivot = row(cols[0], 0)
        for p in range(8):
            r = reciprocal(pivot)
            if p < 7:
                ahead = row(cols[p + 1], p)
                pivot = row(cols[p + 1], p + 1) - (row(cols[p], p + 1) * ahead) * r
            for j in range(p + 1, 8):
                u = (ahead if j == p + 1 else row(cols[j], p)) * r
                cols[j] = jnp.where(is_row[p], u, cols[j] - cols[p] * u)
            u = row(out, p) * r
            out = jnp.where(is_row[p], u, out - cols[p] * u)
        pivots = [row(out, c) for c in range(8)]
        order = [k + 1] if k + 1 < strips else []
        for i in order + [i for i in range(strips) if i not in (k, k + 1)]:
            terms = [column(strip[i], first + c) * pivots[c] for c in range(8)]
            strip[i] = jnp.where(inside, 0.0, strip[i]) - tree(terms)
        strip[k] = out
    for i in range(strips):
        m_ref[8 * i : 8 * i + 8, :] = strip[i]


def invert(a_ref, leaf_ref):
    n = a_ref.shape[0]

    @pl.loop(0, n // LEAF)
    def _(k):
        here = pl.ds(pl.multiple_of(k * LEAF, LEAF), LEAF)
        leaf_ref[...] = a_ref[here, here]
        leaf_inverse(leaf_ref)
        inverse = leaf_ref[...]
        a_ref[here, here] = jnp.zeros((LEAF, LEAF), F32)
        across = mm_full(inverse, a_ref[here, :])
        down = a_ref[:, here]
        a_ref[...] = a_ref[...] - mm_full(down, across)
        a_ref[:, here] = -mm_full(down, inverse)
        a_ref[here, :] = across
        a_ref[here, here] = inverse


def add_diagonal(x, diagonal):
    rows = lax.broadcasted_iota(jnp.int32, x.shape, 0)
    columns = lax.broadcasted_iota(jnp.int32, x.shape, 1)
    return x + jnp.where(rows == columns, diagonal, 0.0)


def client_kernel(
    x_ref, r_ref, g_ref, t_ref, prior_ref, tri_ref, rest_ref, corner_ref, z_ref, a_ref, leaf_ref
):
    x = x_ref[...]
    x_t = x.T
    a_ref[...] = add_diagonal(mm(x_t, x), prior_ref[...])
    invert(a_ref, leaf_ref)
    a_high, a_low = split(a_ref[...])
    width_r, width_g = r_ref.shape[1], g_ref.shape[1]
    r_t, g_t = r_ref[...].T, g_ref[...].T
    step = 256

    def reduced(data, at):
        c_high, c_low = split(mm(x_t, data))
        z = mm(a_high, c_high) + (mm(a_high, c_low) + mm(a_low, c_high))
        z_ref[:, at : at + step] = z
        z_high, z_low = split(z)
        return split(data.astype(F32) - (mm(x, z_high) + mm(x, z_low)))

    slot = 0
    for at in range(0, width_r, step):
        high, low = reduced(r_ref[:, at : at + step], at)
        left = r_t[: at + step]
        block = mm(left, high) + mm(left, low)
        for j in range(at // LEAF, (at + step) // LEAF):
            lo = j * LEAF - at
            tri_ref[slot * LEAF : (slot + j + 1) * LEAF, :] = block[: (j + 1) * LEAF, lo : lo + LEAF]
            slot += j + 1
    done = width_r
    for data_ref in (g_ref, t_ref):
        for at in range(0, data_ref.shape[1], step):
            high, low = reduced(data_ref[:, at : at + step], done)
            block = mm(r_t, high) + mm(r_t, low)
            for lo in range(0, step, LEAF):
                row = (done - width_r + lo) // LEAF * width_r
                rest_ref[row : row + width_r, :] = block[:, lo : lo + LEAF]
            corner_ref[:, done - width_r : done - width_r + step] = mm(g_t, high) + mm(g_t, low)
            done += step


def region_kernel(
    tri_ref, rest_ref, corner_ref, prior_ref, zr_ref, term_ref, a_ref, b_ref, leaf_ref
):
    n = a_ref.shape[0]
    slot = 0
    for j in range(n // LEAF):
        for i in range(j + 1):
            block = tri_ref[slot * LEAF : (slot + 1) * LEAF, :]
            a_ref[i * LEAF : (i + 1) * LEAF, j * LEAF : (j + 1) * LEAF] = block
            if i < j:
                a_ref[j * LEAF : (j + 1) * LEAF, i * LEAF : (i + 1) * LEAF] = block.T
            slot += 1
    a_ref[...] = add_diagonal(a_ref[...], prior_ref[...])
    invert(a_ref, leaf_ref)
    total = zr_ref.shape[1]
    for j in range(total // LEAF):
        b_ref[:, j * LEAF : (j + 1) * LEAF] = rest_ref[j * n : (j + 1) * n, :]
    zr_ref[...] = mm3(a_ref[...], b_ref[...])
    width_g = corner_ref.shape[0]
    share = n // (SIDE * SIDE)
    mine = pl.ds(pl.multiple_of(lax.axis_index("client") * share, share), share)
    term = corner_ref[...] - mm_full(b_ref[mine, :width_g].T, zr_ref[mine, :])
    for j in range(total // LEAF):
        term_ref[j * width_g : (j + 1) * width_g, :] = term[:, j * LEAF : (j + 1) * LEAF]


def back_kernel(
    total_ref, prior_ref, zr_ref, z_ref, private_ref, reg_ref, glob_ref, h_ref, full_ref, leaf_ref
):
    width_g = h_ref.shape[0]
    width_r = zr_ref.shape[0]
    blocks = width_g // LEAF
    block = lambda j: total_ref[j * width_g : (j + 1) * width_g, :]
    h_ref[...] = add_diagonal(
        jnp.concatenate([block(j) for j in range(blocks)], axis=1), prior_ref[...]
    )
    invert(h_ref, leaf_ref)
    rhs = jnp.concatenate(
        [block(j) for j in range(blocks, total_ref.shape[0] // width_g)], axis=1
    )
    glob = mm3(h_ref[...], rhs)
    regional = zr_ref[:, width_g:] - mm3(zr_ref[:, :width_g], glob)
    full_ref[:width_r, :] = regional
    full_ref[width_r:, :] = glob
    side = width_r + width_g
    private_ref[...] = z_ref[:, side:] - mm3(z_ref[:, :side], full_ref[...])
    share = reg_ref.shape[0]
    at = pl.multiple_of(lax.axis_index("client") * share, share)
    reg_ref[...] = full_ref[pl.ds(at, share), :]
    share = glob_ref.shape[0]
    at = pl.multiple_of(width_r + lax.axis_index("region") * share, share)
    glob_ref[...] = full_ref[pl.ds(at, share), :]


class Copies:
    def __init__(self, send_sem, recv_sem):
        self.send_sem, self.recv_sem, self.used, self.sent = send_sem, recv_sem, 0, []

    def put(self, src, dst, peer):
        copy = pltpu.make_async_remote_copy(
            src_ref=src,
            dst_ref=dst,
            send_sem=self.send_sem.at[self.used],
            recv_sem=self.recv_sem.at[self.used],
            device_id=peer,
            device_id_type=MESH,
        )
        self.used += 1
        copy.start()
        self.sent.append(copy)
        return copy

    def finish(self):
        for copy in self.sent:
            copy.wait_send()


def half_of(rows):
    return (rows // 2 + 7) // 8 * 8


def ring_sum(copies, src, base, rows, here, right, left, scratch, write):
    cut = half_of(rows)
    rest = rows - cut
    from_left, from_right, far_right, far_left, give_right, give_left = scratch

    def piece(i, at, size):
        start = base + lax.rem(here + i, SIDE) * rows + at
        return src.at[pl.ds(pl.multiple_of(start, 8), size), :]

    a = copies.put(piece(2, 0, cut), far_right.at[pl.ds(0, cut), :], right)
    b = copies.put(piece(2, cut, rest), far_left.at[pl.ds(0, rest), :], left)
    c = copies.put(piece(1, cut, rest), from_left.at[pl.ds(cut, rest), :], right)
    d = copies.put(piece(3, 0, cut), from_right.at[pl.ds(0, cut), :], left)
    yield
    a.wait_recv()
    give_right[...] = piece(1, 0, cut)[...] + far_right[...]
    e = copies.put(give_right, from_left.at[pl.ds(0, cut), :], right)
    b.wait_recv()
    give_left[...] = piece(3, cut, rest)[...] + far_left[...]
    f = copies.put(give_left, from_right.at[pl.ds(cut, rest), :], left)
    yield
    c.wait_recv()
    e.wait_recv()
    d.wait_recv()
    f.wait_recv()
    write(piece(0, 0, rows)[...] + (from_left[...] + from_right[...]))


def ring_spread(copies, out, base, rows, here, right, left):
    cut = half_of(rows)
    rest = rows - cut

    def piece(i, at, size):
        start = base + lax.rem(here + i, SIDE) * rows + at
        return out.at[pl.ds(pl.multiple_of(start, 8), size), :]

    own = piece(0, 0, rows)
    a = copies.put(own, own, right)
    b = copies.put(own, own, left)
    yield
    a.wait_recv()
    part = piece(3, 0, cut)
    c = copies.put(part, part, right)
    b.wait_recv()
    part = piece(1, cut, rest)
    d = copies.put(part, part, left)
    yield
    c.wait_recv()
    d.wait_recv()


def drive(tasks):
    tasks = list(tasks)
    while tasks:
        alive = []
        for task in tasks:
            try:
                next(task)
                alive.append(task)
            except StopIteration:
                pass
        tasks = alive


def neighbours():
    client = lax.axis_index("client")
    x, y = lax.div(client, SIDE), lax.rem(client, SIDE)

    def peer(dx, dy):
        return {"client": lax.rem(x + dx, SIDE) * SIDE + lax.rem(y + dy, SIDE)}

    return (x, peer(1, 0), peer(SIDE - 1, 0)), (y, peer(0, 1), peer(0, SIDE - 1))


def pair_scratch(rows):
    shapes = []
    for size in (rows // 8, rows // 32):
        cut = half_of(size)
        for n in (size, size, cut, size - cut, cut, size - cut):
            shapes.append(pltpu.VMEM((n, LEAF), F32))
    shapes.append(pltpu.VMEM((rows // 8, LEAF), F32))
    return shapes


SCRATCHES = 13


def half_reduce(copies, src, rows, half, first, second, scratch, write):
    big, small = rows // 8, rows // 32
    mid = scratch[12]

    def keep(v):
        mid[...] = v

    yield from ring_sum(copies, src, half * (rows // 2), big, *first, scratch[:6], keep)
    yield from ring_sum(copies, mid, 0, small, *second, scratch[6:12], write)


def half_spread(copies, out, rows, half, first, second):
    big, small = rows // 8, rows // 32
    base = half * (rows // 2)
    yield from ring_spread(copies, out, base + first[0] * big, small, *second)
    yield from ring_spread(copies, out, base, big, *first)


def own_rows(rows, half, first, second):
    start = half * (rows // 2) + first[0] * (rows // 8) + second[0] * (rows // 32)
    return pl.ds(pl.multiple_of(start, 8), rows // 32)


def greet(peers):
    barrier = pltpu.get_barrier_semaphore()
    for peer in peers:
        pl.semaphore_signal(barrier, inc=1, device_id=peer, device_id_type=MESH)
    pl.semaphore_wait(barrier, len(peers))


def plane_sum_kernel(count, *refs):
    srcs, outs = refs[:count], refs[count : 2 * count]
    scratch = refs[2 * count : -2]
    copies = Copies(*refs[-2:])
    axes = neighbours()
    greet([peer for axis in axes for peer in axis[1:]])
    tasks = []
    for i, (src, out) in enumerate(zip(srcs, outs)):
        rows = src.shape[0]
        for half in range(2):
            first, second = axes[half], axes[1 - half]
            mine = scratch[(2 * i + half) * SCRATCHES : (2 * i + half + 1) * SCRATCHES]

            def task(src=src, out=out, rows=rows, half=half, first=first, second=second, mine=mine):
                def write(v):
                    out[own_rows(rows, half, first, second), :] = v

                yield from half_reduce(copies, src, rows, half, first, second, mine, write)
                yield from half_spread(copies, out, rows, half, first, second)

            tasks.append(task())
    drive(tasks)
    copies.finish()


def plane_sum(arrays):
    scratch = []
    for array in arrays:
        scratch += pair_scratch(array.shape[0]) * 2
    sems = 40 * len(arrays)
    return pl.pallas_call(
        functools.partial(plane_sum_kernel, len(arrays)),
        out_shape=[jax.ShapeDtypeStruct(a.shape, F32) for a in arrays],
        in_specs=[VMEM] * len(arrays),
        out_specs=[VMEM] * len(arrays),
        scratch_shapes=scratch
        + [pltpu.SemaphoreType.DMA((sems,)), pltpu.SemaphoreType.DMA((sems,))],
        compiler_params=pltpu.CompilerParams(collective_id=0, has_side_effects=True),
        name="plane_sum",
    )(*arrays)


def slice_sum_kernel(depth, src, out, *refs):
    scratch, copies = refs[: 2 * SCRATCHES], Copies(*refs[-2:])
    keep, got, inbox, tile, final = refs[2 * SCRATCHES : -2]
    rows = src.shape[0]
    axes = neighbours()
    region = lax.axis_index("region")
    z, core = lax.div(region, 2), lax.rem(region, 2)
    other = {"region": z * 2 + 1 - core}

    def along(dz):
        return {"region": lax.rem(z + dz, depth) * 2 + core}

    column = [along(d) for d in range(1, depth)]
    greet([peer for axis in axes for peer in axis[1:]] + [other] + column)
    piece = rows // 32

    def task(half):
        first, second = axes[half], axes[1 - half]
        mine = scratch[half * SCRATCHES : (half + 1) * SCRATCHES]

        def write(v):
            keep[half] = v

        return half_reduce(copies, src, rows, half, first, second, mine, write)

    drive([task(0), task(1)])
    swap = copies.put(keep.at[1 - core], got, other)
    swap.wait_recv()
    keep_sum = keep[core] + got[...]
    tiles = piece // 8
    for t in range(tiles):
        tile[t] = keep_sum[8 * t : 8 * t + 8]
    sent = []
    for d in range(1, depth):
        sent.append(copies.put(tile.at[lax.rem(z + d, tiles)], inbox.at[d - 1], along(d)))
    for copy in sent:
        copy.wait_recv()
    me = lax.rem(z, tiles)
    final[me] = tree([tile[me]] + [inbox[d] for d in range(depth - 1)])
    group = z - me
    sent = []
    for d in range(1, tiles):
        peer = {"region": (group + lax.rem(me + d, tiles)) * 2 + core}
        sent.append(copies.put(final.at[me], final.at[me], peer))
    for copy in sent:
        copy.wait_recv()
    value = jnp.concatenate([final[t] for t in range(tiles)], axis=0)
    where = [own_rows(rows, half, axes[half], axes[1 - half]) for half in range(2)]
    keep_final = got
    for half in range(2):

        @pl.when(core == half)
        def _():
            out[where[half], :] = value

    del keep_final
    start = [w.start for w in where]
    mine_at = jnp.where(core == 0, start[0], start[1])
    mine = out.at[pl.ds(pl.multiple_of(mine_at, 8), piece), :]
    copies.put(mine, mine, other).wait_recv()
    drive(
        half_spread(copies, out, rows, half, axes[half], axes[1 - half]) for half in range(2)
    )
    copies.finish()


def slice_sum(array, depth):
    rows = array.shape[0]
    piece = rows // 32
    sems = 64
    return pl.pallas_call(
        functools.partial(slice_sum_kernel, depth),
        out_shape=jax.ShapeDtypeStruct(array.shape, F32),
        in_specs=[VMEM],
        out_specs=VMEM,
        scratch_shapes=pair_scratch(rows) * 2
        + [
            pltpu.VMEM((2, piece, LEAF), F32),
            pltpu.VMEM((piece, LEAF), F32),
            pltpu.VMEM((depth - 1, 8, LEAF), F32),
            pltpu.VMEM((piece // 8, 8, LEAF), F32),
            pltpu.VMEM((piece // 8, 8, LEAF), F32),
            pltpu.SemaphoreType.DMA((sems,)),
            pltpu.SemaphoreType.DMA((sems,)),
        ],
        compiler_params=pltpu.CompilerParams(collective_id=1, has_side_effects=True),
        name="slice_sum",
    )(array)


def dense(kernel, shapes, scratch, name):
    return pl.pallas_call(
        kernel,
        out_shape=[jax.ShapeDtypeStruct(s, F32) for s in shapes],
        out_specs=[VMEM] * len(shapes),
        scratch_shapes=[pltpu.VMEM(s, F32) for s in scratch],
        name=name,
    )


def eliminate_client(x, r, g, t, prior):
    p, width_r, width_g, rhs = x.shape[1], r.shape[1], g.shape[1], t.shape[1]
    blocks = width_r // LEAF
    rest = width_g + rhs
    return dense(
        client_kernel,
        [
            (blocks * (blocks + 1) // 2 * LEAF, LEAF),
            (width_r * rest // LEAF, LEAF),
            (width_g, rest),
            (p, width_r + rest),
        ],
        [(p, p), (LEAF, LEAF)],
        "eliminate_client",
    )(x, r, g, t, prior)


def eliminate_region(tri, rest, corner, prior):
    width_r, (width_g, total) = prior.shape[1], corner.shape
    return dense(
        region_kernel,
        [(width_r, total), (width_g * total // LEAF, LEAF)],
        [(width_r, width_r), (width_r, total), (LEAF, LEAF)],
        "eliminate_region",
    )(tri, rest, corner, prior)


def substitute(total, prior, zr, z, regions):
    width_r, width_g, p = zr.shape[0], prior.shape[1], z.shape[0]
    rhs = zr.shape[1] - width_g
    return dense(
        back_kernel,
        [(p, rhs), (width_r // (SIDE * SIDE), rhs), (width_g // regions, rhs)],
        [(width_g, width_g), (width_r + width_g, rhs), (LEAF, LEAF)],
        "substitute",
    )(total, prior, zr, z)


def solution(mesh):
    regions = mesh.shape["region"]

    def per_device(x, r, g, t, private_prior, regional_prior, global_prior):
        tri, rest, corner, z = eliminate_client(
            x[0, 0], r[0, 0], g[0, 0], t[0, 0], private_prior[0]
        )
        tri, rest = plane_sum([tri, rest])
        zr, term = eliminate_region(tri, rest, corner, regional_prior)
        total = slice_sum(term, regions // 2)
        private, regional, glob = substitute(total, global_prior[None], zr, z, regions)
        return private[None, None], regional[None], glob

    placed = (
        P("region", "client", None, None),
        P("region", "client", None, None),
        P("region", "client", None, None),
        P("region", "client", None, None),
        P("region", "client", None),
        P("region", None),
        P(),
    )
    return jax.shard_map(
        per_device,
        mesh=mesh,
        in_specs=placed,
        out_specs=(
            P("region", "client", None, None),
            P("region", "client", None),
            P("region", None),
        ),
        check_vma=False,
    )
```

```python
import functools

import jax
import jax.numpy as jnp
from jax import lax
from jax.experimental import pallas as pl
from jax.experimental.pallas import tpu as pltpu
from jax.sharding import PartitionSpec as P

F32 = jnp.float32
BF16 = jnp.bfloat16
MESH = pl.DeviceIdType.MESH
HIGHEST = lax.Precision.HIGHEST
LEAF = 128
SIDE = 4
VMEM = pl.BlockSpec(memory_space=pltpu.VMEM)


def split(x):
    high = x.astype(BF16)
    return high, (x - high.astype(F32)).astype(BF16)


def mm(a, b):
    return jnp.dot(a, b, preferred_element_type=F32)


def mm3(a, b):
    a_high, a_low = split(a)
    b_high, b_low = split(b)
    return mm(
        jnp.concatenate([a_high, a_high, a_low], axis=1),
        jnp.concatenate([b_high, b_low, b_high], axis=0),
    )


def mm2(a, b):
    b_high, b_low = split(b)
    return mm(jnp.concatenate([a, a], axis=1), jnp.concatenate([b_high, b_low], axis=0))


def mm_full(a, b):
    return jnp.dot(a, b, preferred_element_type=F32, precision=HIGHEST)


def tree(terms):
    while len(terms) > 1:
        terms = [
            terms[i] + terms[i + 1] if i + 1 < len(terms) else terms[i]
            for i in range(0, len(terms), 2)
        ]
    return terms[0]


def leaf_inverse(m_ref):
    n = LEAF
    strips = n // 8
    lane = lax.broadcasted_iota(jnp.int32, (8, n), 1)
    sub = lax.broadcasted_iota(jnp.int32, (8, n), 0)
    is_row = [sub == k for k in range(8)]

    def row(v, k):
        return jnp.broadcast_to(v[k : k + 1, :], (8, n))

    def column(v, l):
        return jnp.broadcast_to(v[:, l : l + 1], (8, n))

    strip = [m_ref[8 * i : 8 * i + 8, :] for i in range(strips)]
    for k in range(strips):
        first = 8 * k
        cols = [column(strip[k], first + c) for c in range(8)]
        inside = (lane >= first) & (lane < first + 8)
        out = jnp.where(inside, jnp.where(lane - first == sub, 1.0, 0.0), strip[k])
        pivot = row(cols[0], 0)
        for p in range(8):
            r = pltpu.reciprocal(pivot, approx=True)
            if p < 7:
                ahead = row(cols[p + 1], p)
                pivot = row(cols[p + 1], p + 1) - (row(cols[p], p + 1) * ahead) * r
            for j in range(p + 1, 8):
                u = (ahead if j == p + 1 else row(cols[j], p)) * r
                cols[j] = jnp.where(is_row[p], u, cols[j] - cols[p] * u)
            u = row(out, p) * r
            out = jnp.where(is_row[p], u, out - cols[p] * u)
        pivots = [row(out, c) for c in range(8)]
        order = [k + 1] if k + 1 < strips else []
        for i in order + [i for i in range(strips) if i not in (k, k + 1)]:
            terms = [column(strip[i], first + c) * pivots[c] for c in range(8)]
            strip[i] = jnp.where(inside, 0.0, strip[i]) - tree(terms)
        strip[k] = out
    for i in range(strips):
        m_ref[8 * i : 8 * i + 8, :] = strip[i]


def invert(a_ref, leaf_ref):
    n = a_ref.shape[0]

    @pl.loop(0, n // LEAF)
    def _(k):
        here = pl.ds(pl.multiple_of(k * LEAF, LEAF), LEAF)
        leaf_ref[...] = a_ref[here, here]
        leaf_inverse(leaf_ref)
        inverse = leaf_ref[...]
        down = a_ref[:, here]
        a_ref[here, :] = mm3(inverse, a_ref[here, :])
        a_ref[here, here] = inverse
        across = a_ref[here, :]
        a_ref[:, here] = jnp.zeros((n, LEAF), F32)
        a_ref[...] = a_ref[...] - mm3(down, across)
        a_ref[here, :] = across


def add_diagonal(x, diagonal):
    rows = lax.broadcasted_iota(jnp.int32, x.shape, 0)
    columns = lax.broadcasted_iota(jnp.int32, x.shape, 1)
    return x + jnp.where(rows == columns, diagonal, 0.0)


def client_part(x_ref, r_ref, g_ref, t_ref, prior_ref, tri_ref, rest_ref, corner_ref, z_ref, a_ref, leaf_ref):
    x = x_ref[...]
    x_t = x.T
    a_ref[...] = add_diagonal(mm(x_t, x), prior_ref[...])
    invert(a_ref, leaf_ref)
    a_high, a_low = split(a_ref[...])
    a_three = jnp.concatenate([a_high, a_high, a_low], axis=1)
    x_two = jnp.concatenate([x, x], axis=1)
    width_r = r_ref.shape[1]
    r_t, g_t = r_ref[...].T, g_ref[...].T
    step = 256

    def reduced(data, at):
        c_high, c_low = split(mm(x_t, data))
        z = mm(a_three, jnp.concatenate([c_high, c_low, c_high], axis=0))
        z_ref[:, at : at + step] = z
        return data.astype(F32) - mm(x_two, jnp.concatenate(split(z), axis=0))

    slot = 0
    for at in range(0, width_r, step):
        block = mm2(r_t[: at + step], reduced(r_ref[:, at : at + step], at))
        for j in range(at // LEAF, (at + step) // LEAF):
            lo = j * LEAF - at
            tri_ref[slot * LEAF : (slot + j + 1) * LEAF, :] = block[: (j + 1) * LEAF, lo : lo + LEAF]
            slot += j + 1
    done = width_r
    for data_ref in (g_ref, t_ref):
        for at in range(0, data_ref.shape[1], step):
            residual = reduced(data_ref[:, at : at + step], done)
            block = mm2(r_t, residual)
            for lo in range(0, step, LEAF):
                row = (done - width_r + lo) // LEAF * width_r
                rest_ref[row : row + width_r, :] = block[:, lo : lo + LEAF]
            corner_ref[:, done - width_r : done - width_r + step] = mm2(g_t, residual)
            done += step


def region_block(tri_ref, prior_ref, a_ref):
    slot = 0
    for j in range(a_ref.shape[0] // LEAF):
        for i in range(j + 1):
            block = tri_ref[slot * LEAF : (slot + 1) * LEAF, :]
            a_ref[i * LEAF : (i + 1) * LEAF, j * LEAF : (j + 1) * LEAF] = block
            if i < j:
                a_ref[j * LEAF : (j + 1) * LEAF, i * LEAF : (i + 1) * LEAF] = block.T
            slot += 1
    a_ref[...] = add_diagonal(a_ref[...], prior_ref[...])


def region_term(client, rest_ref, corner_ref, zr_ref, term_ref, a_ref, b_ref):
    n = a_ref.shape[0]
    total = zr_ref.shape[1]
    for j in range(total // LEAF):
        b_ref[:, j * LEAF : (j + 1) * LEAF] = rest_ref[j * n : (j + 1) * n, :]
    zr_ref[...] = mm3(a_ref[...], b_ref[...])
    width_g = corner_ref.shape[0]
    share = n // (SIDE * SIDE)
    mine = pl.ds(pl.multiple_of(client * share, share), share)
    term = corner_ref[...] - mm_full(b_ref[mine, :width_g].T, zr_ref[mine, :])
    for j in range(total // LEAF):
        term_ref[j * width_g : (j + 1) * width_g, :] = term[:, j * LEAF : (j + 1) * LEAF]


def back_part(client, region, total_ref, prior_ref, zr_ref, z_ref, private_ref, reg_ref, glob_ref, h_ref, full_ref, leaf_ref):
    width_g = h_ref.shape[0]
    width_r = zr_ref.shape[0]
    blocks = width_g // LEAF

    def block(j):
        return total_ref[j * width_g : (j + 1) * width_g, :]

    h_ref[...] = add_diagonal(
        jnp.concatenate([block(j) for j in range(blocks)], axis=1), prior_ref[...]
    )
    invert(h_ref, leaf_ref)
    rhs = jnp.concatenate(
        [block(j) for j in range(blocks, total_ref.shape[0] // width_g)], axis=1
    )
    glob = mm3(h_ref[...], rhs)
    regional = zr_ref[:, width_g:] - mm3(zr_ref[:, :width_g], glob)
    full_ref[:width_r, :] = regional
    full_ref[width_r:, :] = glob
    side = width_r + width_g
    private_ref[...] = z_ref[:, side:] - mm3(z_ref[:, :side], full_ref[...])
    share = reg_ref.shape[0]
    reg_ref[...] = full_ref[pl.ds(pl.multiple_of(client * share, share), share), :]
    share = glob_ref.shape[0]
    glob_ref[...] = full_ref[pl.ds(pl.multiple_of(width_r + region * share, share), share), :]


class Copies:
    def __init__(self, send_sem, recv_sem):
        self.send_sem, self.recv_sem, self.used, self.sent = send_sem, recv_sem, 0, []

    def put(self, src, dst, peer):
        copy = pltpu.make_async_remote_copy(
            src_ref=src,
            dst_ref=dst,
            send_sem=self.send_sem.at[self.used],
            recv_sem=self.recv_sem.at[self.used],
            device_id=peer,
            device_id_type=MESH,
        )
        self.used += 1
        copy.start()
        self.sent.append(copy)
        return copy

    def finish(self):
        for copy in self.sent:
            copy.wait_send()


def half_of(rows):
    return (rows // 2 + 7) // 8 * 8


def ring_sum(copies, src, base, rows, here, right, left, scratch, write):
    cut = half_of(rows)
    rest = rows - cut
    from_left, from_right, far_right, far_left, give_right, give_left = scratch

    def piece(i, at, size):
        start = base + lax.rem(here + i, SIDE) * rows + at
        return src.at[pl.ds(pl.multiple_of(start, 8), size), :]

    a = copies.put(piece(2, 0, cut), far_right.at[pl.ds(0, cut), :], right)
    b = copies.put(piece(2, cut, rest), far_left.at[pl.ds(0, rest), :], left)
    c = copies.put(piece(1, cut, rest), from_left.at[pl.ds(cut, rest), :], right)
    d = copies.put(piece(3, 0, cut), from_right.at[pl.ds(0, cut), :], left)
    yield
    a.wait_recv()
    give_right[...] = piece(1, 0, cut)[...] + far_right[...]
    e = copies.put(give_right, from_left.at[pl.ds(0, cut), :], right)
    b.wait_recv()
    give_left[...] = piece(3, cut, rest)[...] + far_left[...]
    f = copies.put(give_left, from_right.at[pl.ds(cut, rest), :], left)
    yield
    c.wait_recv()
    e.wait_recv()
    d.wait_recv()
    f.wait_recv()
    write(piece(0, 0, rows)[...] + (from_left[...] + from_right[...]))


def ring_spread(copies, out, base, rows, here, right, left):
    cut = half_of(rows)
    rest = rows - cut

    def piece(i, at, size):
        start = base + lax.rem(here + i, SIDE) * rows + at
        return out.at[pl.ds(pl.multiple_of(start, 8), size), :]

    own = piece(0, 0, rows)
    a = copies.put(own, own, right)
    b = copies.put(own, own, left)
    yield
    a.wait_recv()
    part = piece(3, 0, cut)
    c = copies.put(part, part, right)
    b.wait_recv()
    part = piece(1, cut, rest)
    d = copies.put(part, part, left)
    yield
    c.wait_recv()
    d.wait_recv()


def drive(tasks):
    tasks = list(tasks)
    while tasks:
        alive = []
        for task in tasks:
            try:
                next(task)
                alive.append(task)
            except StopIteration:
                pass
        tasks = alive


def later(rounds, task):
    for _ in range(rounds):
        yield
    yield from task


def sum_scratch(rows):
    shapes = []
    for size in (rows // 4, rows // 16):
        cut = half_of(size)
        for n in (size, size, cut, size - cut, cut, size - cut):
            shapes.append((n, LEAF))
    shapes.append((rows // 4, LEAF))
    return shapes


SCRATCHES = 13


def plane_reduce(copies, src, base, rows, first, second, scratch, write):
    mid = scratch[12]

    def keep(v):
        mid[...] = v

    yield from ring_sum(copies, src, base, rows // 4, *first, scratch[:6], keep)
    yield from ring_sum(copies, mid, 0, rows // 16, *second, scratch[6:12], write)


def plane_spread(copies, out, base, rows, first, second):
    yield from ring_spread(copies, out, base + first[0] * (rows // 4), rows // 16, *second)
    yield from ring_spread(copies, out, base, rows // 4, *first)


def own_rows(base, rows, first, second):
    start = base + first[0] * (rows // 4) + second[0] * (rows // 16)
    return pl.ds(pl.multiple_of(start, 8), rows // 16)


def solve_kernel(
    depth,
    x_ref,
    r_ref,
    g_ref,
    t_ref,
    private_prior,
    regional_prior,
    global_prior,
    private_ref,
    reg_ref,
    glob_ref,
    a_ref,
    leaf_ref,
    z_ref,
    tri_src,
    rest_src,
    corner_ref,
    tri_ref,
    rest_ref,
    b_ref,
    zr_ref,
    term_ref,
    total_ref,
    h_ref,
    full_ref,
    swap,
    pair,
    inbox,
    tile,
    final,
    *refs,
):
    scratch, copies = refs[:-2], Copies(*refs[-2:])
    client, region = lax.axis_index("client"), lax.axis_index("region")
    x, y = lax.div(client, SIDE), lax.rem(client, SIDE)
    z, core = lax.div(region, 2), lax.rem(region, 2)

    def shifted(dx, dy):
        return lax.rem(x + dx, SIDE) * SIDE + lax.rem(y + dy, SIDE)

    def above(dz):
        return {"region": lax.rem(z + dz, depth) * 2 + core}

    x_line = (x, {"client": shifted(1, 0)}, {"client": shifted(SIDE - 1, 0)})
    y_line = (y, {"client": shifted(0, 1)}, {"client": shifted(0, SIDE - 1)})
    plane = [{"client": lax.rem(client + d, SIDE * SIDE)} for d in range(1, SIDE * SIDE)]
    other = {"region": z * 2 + 1 - core}
    column = [above(d) for d in range(1, depth)]
    peers = plane + column + [other]
    barrier = pltpu.get_barrier_semaphore()
    for peer in peers:
        pl.semaphore_signal(barrier, inc=1, device_id=peer, device_id_type=MESH)

    client_part(
        x_ref, r_ref, g_ref, t_ref, private_prior, tri_src, rest_src, corner_ref, z_ref, a_ref, leaf_ref
    )
    pl.semaphore_wait(barrier, len(peers))

    halves = [(x_line, y_line), (y_line, x_line)]

    def region_sum(i, half, src, out, spread):
        rows = src.shape[0] // 2
        base = half * rows
        first, second = halves[half]
        mine = scratch[(2 * i + half) * SCRATCHES : (2 * i + half + 1) * SCRATCHES]

        def write(v):
            out[own_rows(base, rows, first, second), :] = v

        yield from plane_reduce(copies, src, base, rows, first, second, mine, write)
        if spread:
            yield from plane_spread(copies, out, base, rows, first, second)

    tasks = [region_sum(0, half, tri_src, tri_ref, True) for half in range(2)]
    tasks += [later(2, region_sum(1, half, rest_src, rest_ref, False)) for half in range(2)]
    drive(tasks)
    spreading = []
    for half in range(2):
        rows = rest_ref.shape[0] // 2
        own = rest_ref.at[own_rows(half * rows, rows, *halves[half]), :]
        for peer in plane:
            spreading.append(copies.put(own, own, peer))
    region_block(tri_ref, regional_prior, a_ref)
    invert(a_ref, leaf_ref)
    for copy in spreading:
        copy.wait_recv()
    region_term(client, rest_ref, corner_ref, zr_ref, term_ref, a_ref, b_ref)

    rows = term_ref.shape[0] // 2
    base = pl.multiple_of(core * rows, 8)
    away = term_ref.at[pl.ds(pl.multiple_of((1 - core) * rows, 8), rows), :]
    copies.put(away, swap, other).wait_recv()
    pair[...] = term_ref[pl.ds(base, rows), :] + swap[...]

    def choose(a, b):
        pick = lambda u, v: jnp.where(core == 0, u, v)
        return (
            pick(a[0], b[0]),
            {"client": pick(a[1]["client"], b[1]["client"])},
            {"client": pick(a[2]["client"], b[2]["client"])},
        )

    first, second = choose(x_line, y_line), choose(y_line, x_line)
    tiles = rows // 16 // 8

    def write_tiles(v):
        for t in range(tiles):
            tile[t] = v[8 * t : 8 * t + 8]

    drive(
        [plane_reduce(copies, pair, 0, rows, first, second, scratch[4 * SCRATCHES :], write_tiles)]
    )
    sent = []
    for d in range(1, depth):
        sent.append(copies.put(tile.at[lax.rem(z + d, tiles)], inbox.at[d - 1], above(d)))
    for copy in sent:
        copy.wait_recv()
    me = lax.rem(z, tiles)
    final[me] = tree([tile[me]] + [inbox[d] for d in range(depth - 1)])
    sent = []
    for d in range(1, tiles):
        peer = {"region": (z - me + lax.rem(me + d, tiles)) * 2 + core}
        sent.append(copies.put(final.at[me], final.at[me], peer))
    for copy in sent:
        copy.wait_recv()
    value = jnp.concatenate([final[t] for t in range(tiles)], axis=0)
    total_ref[own_rows(base, rows, first, second), :] = value
    drive([plane_spread(copies, total_ref, base, rows, first, second)])
    mine = total_ref.at[pl.ds(base, rows), :]
    copies.put(mine, mine, other).wait_recv()

    back_part(
        client, region, total_ref, global_prior, zr_ref, z_ref, private_ref, reg_ref, glob_ref, h_ref, full_ref, leaf_ref
    )
    copies.finish()


def solve(x, r, g, t, private_prior, regional_prior, global_prior, regions):
    p, width_r, width_g, rhs = x.shape[1], r.shape[1], g.shape[1], t.shape[1]
    depth, clients = regions // 2, SIDE * SIDE
    blocks = width_r // LEAF
    rest = width_g + rhs
    tri_rows = blocks * (blocks + 1) // 2 * LEAF
    rest_rows = width_r * rest // LEAF
    term_rows = width_g * rest // LEAF
    tiles = term_rows // 2 // clients // 8
    shapes = [
        (max(p, width_r), max(p, width_r)),
        (LEAF, LEAF),
        (p, width_r + rest),
        (tri_rows, LEAF),
        (rest_rows, LEAF),
        (width_g, rest),
        (tri_rows, LEAF),
        (rest_rows, LEAF),
        (width_r, rest),
        (width_r, rest),
        (term_rows, LEAF),
        (term_rows, LEAF),
        (width_g, width_g),
        (width_r + width_g, rhs),
        (term_rows // 2, LEAF),
        (term_rows // 2, LEAF),
        (depth - 1, 8, LEAF),
        (tiles, 8, LEAF),
        (tiles, 8, LEAF),
    ]
    for rows in (tri_rows, rest_rows):
        shapes += sum_scratch(rows // 2) * 2
    shapes += sum_scratch(term_rows // 2)
    sems = 256
    outs = [(p, rhs), (width_r // clients, rhs), (width_g // regions, rhs)]
    return pl.pallas_call(
        functools.partial(solve_kernel, depth),
        out_shape=[jax.ShapeDtypeStruct(s, F32) for s in outs],
        in_specs=[VMEM] * 7,
        out_specs=[VMEM] * len(outs),
        scratch_shapes=[pltpu.VMEM(s, F32) for s in shapes]
        + [pltpu.SemaphoreType.DMA((sems,)), pltpu.SemaphoreType.DMA((sems,))],
        compiler_params=pltpu.CompilerParams(collective_id=0, has_side_effects=True),
        name="solve",
    )(x, r, g, t, private_prior, regional_prior, global_prior)


def solution(mesh):
    regions = mesh.shape["region"]

    def per_device(x, r, g, t, private_prior, regional_prior, global_prior):
        private, regional, glob = solve(
            x[0, 0], r[0, 0], g[0, 0], t[0, 0], private_prior[0], regional_prior, global_prior[None], regions
        )
        return private[None, None], regional[None], glob

    placed = (
        P("region", "client", None, None),
        P("region", "client", None, None),
        P("region", "client", None, None),
        P("region", "client", None, None),
        P("region", "client", None),
        P("region", None),
        P(),
    )
    return jax.shard_map(
        per_device,
        mesh=mesh,
        in_specs=placed,
        out_specs=(
            P("region", "client", None, None),
            P("region", "client", None),
            P("region", None),
        ),
        check_vma=False,
    )
```

```python
import functools

import jax
import jax.numpy as jnp
from jax import lax
from jax.experimental import pallas as pl
from jax.experimental.pallas import tpu as pltpu
from jax.sharding import PartitionSpec as P

F32 = jnp.float32
BF16 = jnp.bfloat16
MESH = pl.DeviceIdType.MESH
HIGHEST = lax.Precision.HIGHEST
LEAF = 128
SIDE = 4
VMEM = pl.BlockSpec(memory_space=pltpu.VMEM)


def split(x):
    high = x.astype(BF16)
    return high, (x - high.astype(F32)).astype(BF16)


def mm(a, b):
    return jnp.dot(a, b, preferred_element_type=F32)


def mm3(a, b):
    a_high, a_low = split(a)
    b_high, b_low = split(b)
    return mm(
        jnp.concatenate([a_high, a_high, a_low], axis=1),
        jnp.concatenate([b_high, b_low, b_high], axis=0),
    )


def mm2(a, b):
    b_high, b_low = split(b)
    return mm(jnp.concatenate([a, a], axis=1), jnp.concatenate([b_high, b_low], axis=0))


def mm_full(a, b):
    return jnp.dot(a, b, preferred_element_type=F32, precision=HIGHEST)


def tree(terms):
    while len(terms) > 1:
        terms = [
            terms[i] + terms[i + 1] if i + 1 < len(terms) else terms[i]
            for i in range(0, len(terms), 2)
        ]
    return terms[0]


def leaf_inverse(m_ref):
    n = LEAF
    strips = n // 8
    lane = lax.broadcasted_iota(jnp.int32, (8, n), 1)
    sub = lax.broadcasted_iota(jnp.int32, (8, n), 0)
    is_row = [sub == k for k in range(8)]

    def row(v, k):
        return jnp.broadcast_to(v[k : k + 1, :], (8, n))

    def column(v, l):
        return jnp.broadcast_to(v[:, l : l + 1], (8, n))

    strip = [m_ref[8 * i : 8 * i + 8, :] for i in range(strips)]
    for k in range(strips):
        first = 8 * k
        cols = [column(strip[k], first + c) for c in range(8)]
        inside = (lane >= first) & (lane < first + 8)
        out = jnp.where(inside, jnp.where(lane - first == sub, 1.0, 0.0), strip[k])
        pivot = row(cols[0], 0)
        for p in range(8):
            r = pltpu.reciprocal(pivot, approx=True)
            if p < 7:
                ahead = row(cols[p + 1], p)
                pivot = row(cols[p + 1], p + 1) - (row(cols[p], p + 1) * ahead) * r
            for j in range(p + 1, 8):
                u = (ahead if j == p + 1 else row(cols[j], p)) * r
                cols[j] = jnp.where(is_row[p], u, cols[j] - cols[p] * u)
            u = row(out, p) * r
            out = jnp.where(is_row[p], u, out - cols[p] * u)
        pivots = [row(out, c) for c in range(8)]
        order = [k + 1] if k + 1 < strips else []
        for i in order + [i for i in range(strips) if i not in (k, k + 1)]:
            terms = [column(strip[i], first + c) * pivots[c] for c in range(8)]
            strip[i] = jnp.where(inside, 0.0, strip[i]) - tree(terms)
        strip[k] = out
    for i in range(strips):
        m_ref[8 * i : 8 * i + 8, :] = strip[i]


def invert(a_ref, leaf_ref, halfway=None):
    n = a_ref.shape[0]

    @pl.loop(0, n // LEAF)
    def _(k):
        if halfway is not None:
            pl.when(k == n // LEAF // 2)(halfway)
        here = pl.ds(pl.multiple_of(k * LEAF, LEAF), LEAF)
        leaf_ref[...] = a_ref[here, here]
        leaf_inverse(leaf_ref)
        inverse = leaf_ref[...]
        down = a_ref[:, here]
        a_ref[here, :] = mm3(inverse, a_ref[here, :])
        a_ref[here, here] = inverse
        across = a_ref[here, :]
        a_ref[:, here] = jnp.zeros((n, LEAF), F32)
        a_ref[...] = a_ref[...] - mm3(down, across)
        a_ref[here, :] = across


def add_diagonal(x, diagonal):
    rows = lax.broadcasted_iota(jnp.int32, x.shape, 0)
    columns = lax.broadcasted_iota(jnp.int32, x.shape, 1)
    return x + jnp.where(rows == columns, diagonal, 0.0)


def client_part(x_ref, r_ref, g_ref, t_ref, prior_ref, tri_ref, rest_ref, corner_ref, z_ref, a_ref, leaf_ref, tri_done):
    x = x_ref[...]
    x_t = x.T
    a_ref[...] = add_diagonal(mm(x_t, x), prior_ref[...])
    invert(a_ref, leaf_ref)
    a_high, a_low = split(a_ref[...])
    a_three = jnp.concatenate([a_high, a_high, a_low], axis=1)
    x_two = jnp.concatenate([x, x], axis=1)
    width_r = r_ref.shape[1]
    r_t, g_t = r_ref[...].T, g_ref[...].T
    step = 256

    def reduced(data, at):
        c_high, c_low = split(mm(x_t, data))
        z = mm(a_three, jnp.concatenate([c_high, c_low, c_high], axis=0))
        z_ref[:, at : at + step] = z
        return data.astype(F32) - mm(x_two, jnp.concatenate(split(z), axis=0))

    slot = 0
    for at in range(0, width_r, step):
        block = mm2(r_t[: at + step], reduced(r_ref[:, at : at + step], at))
        for j in range(at // LEAF, (at + step) // LEAF):
            lo = j * LEAF - at
            tri_ref[slot * LEAF : (slot + j + 1) * LEAF, :] = block[: (j + 1) * LEAF, lo : lo + LEAF]
            slot += j + 1
    tri_done()
    done = width_r
    for data_ref in (g_ref, t_ref):
        for at in range(0, data_ref.shape[1], step):
            residual = reduced(data_ref[:, at : at + step], done)
            block = mm2(r_t, residual)
            for lo in range(0, step, LEAF):
                row = (done - width_r + lo) // LEAF * width_r
                rest_ref[row : row + width_r, :] = block[:, lo : lo + LEAF]
            corner_ref[:, done - width_r : done - width_r + step] = mm2(g_t, residual)
            done += step


def region_block(tri_ref, prior_ref, a_ref):
    slot = 0
    for j in range(a_ref.shape[0] // LEAF):
        for i in range(j + 1):
            block = tri_ref[slot * LEAF : (slot + 1) * LEAF, :]
            a_ref[i * LEAF : (i + 1) * LEAF, j * LEAF : (j + 1) * LEAF] = block
            if i < j:
                a_ref[j * LEAF : (j + 1) * LEAF, i * LEAF : (i + 1) * LEAF] = block.T
            slot += 1
    a_ref[...] = add_diagonal(a_ref[...], prior_ref[...])


def region_term(client, rest_ref, corner_ref, zr_ref, term_ref, a_ref, b_ref):
    n = a_ref.shape[0]
    total = zr_ref.shape[1]
    for j in range(total // LEAF):
        b_ref[:, j * LEAF : (j + 1) * LEAF] = rest_ref[j * n : (j + 1) * n, :]
    zr_ref[...] = mm3(a_ref[...], b_ref[...])
    width_g = corner_ref.shape[0]
    share = n // (SIDE * SIDE)
    mine = pl.ds(pl.multiple_of(client * share, share), share)
    term = corner_ref[...] - mm_full(b_ref[mine, :width_g].T, zr_ref[mine, :])
    for j in range(total // LEAF):
        term_ref[j * width_g : (j + 1) * width_g, :] = term[:, j * LEAF : (j + 1) * LEAF]


def back_part(client, region, total_ref, prior_ref, zr_ref, z_ref, private_ref, reg_ref, glob_ref, h_ref, full_ref, leaf_ref):
    width_g = h_ref.shape[0]
    blocks = width_g // LEAF

    def block(j):
        return total_ref[j * width_g : (j + 1) * width_g, :]

    h_ref[...] = add_diagonal(
        jnp.concatenate([block(j) for j in range(blocks)], axis=1), prior_ref[...]
    )
    invert(h_ref, leaf_ref)
    rhs = jnp.concatenate(
        [block(j) for j in range(blocks, total_ref.shape[0] // width_g)], axis=1
    )
    glob = mm3(h_ref[...], rhs)
    full_ref[...] = glob
    width_r = zr_ref.shape[0]
    ahead = z_ref.at[:, width_r:]
    private_ref[...] = ahead[:, width_g:] - mm3(ahead[:, :width_g], glob)
    share = reg_ref.shape[0]
    mine = pl.ds(pl.multiple_of(client * share, share), share)
    reg_ref[...] = zr_ref[mine, width_g:] - mm3(zr_ref[mine, :width_g], glob)
    share = glob_ref.shape[0]
    glob_ref[...] = full_ref[pl.ds(pl.multiple_of(region * share, share), share), :]


class Copies:
    def __init__(self, send_sem, recv_sem):
        self.send_sem, self.recv_sem, self.made = send_sem, recv_sem, []

    def make(self, src, dst, peer):
        used = len(self.made)
        copy = pltpu.make_async_remote_copy(
            src_ref=src,
            dst_ref=dst,
            send_sem=self.send_sem.at[used],
            recv_sem=self.recv_sem.at[used],
            device_id=peer,
            device_id_type=MESH,
        )
        self.made.append(copy)
        return copy

    def finish(self):
        for copy in self.made:
            copy.wait_send()


def start(copies):
    for copy in copies:
        copy.start()


def arrive(copies):
    for copy in copies:
        copy.wait_recv()


def rows_of(ref, at, rows):
    return ref.at[pl.ds(pl.multiple_of(at, 8), rows), :]


class PlaneSum:
    def __init__(self, copies, client, peers, src, base, rows, inbox):
        self.copies, self.inbox, self.rows, self.peers = copies, inbox, rows, peers
        self.own = rows_of(src, base + client * rows, rows)
        self.at = base + client * rows
        self.scatter = [
            copies.make(rows_of(src, base + peer["client"] * rows, rows), inbox.at[d], peer)
            for d, peer in enumerate(peers)
        ]

    def value(self):
        return tree([self.own[...]] + [self.inbox[d] for d in range(len(self.peers))])

    def gather(self, out):
        self.out = rows_of(out, self.at, self.rows)
        return [self.copies.make(self.out, self.out, peer) for peer in self.peers]


def solve_kernel(
    depth,
    x_ref,
    r_ref,
    g_ref,
    t_ref,
    private_prior,
    regional_prior,
    global_prior,
    private_ref,
    reg_ref,
    glob_ref,
    a_ref,
    leaf_ref,
    z_ref,
    tri_src,
    rest_src,
    corner_ref,
    tri_ref,
    rest_ref,
    b_ref,
    zr_ref,
    term_ref,
    total_ref,
    h_ref,
    full_ref,
    swap,
    pair,
    inbox,
    tile,
    final,
    tri_inbox,
    rest_inbox,
    term_inbox,
    send_sem,
    recv_sem,
):
    copies = Copies(send_sem, recv_sem)
    client, region = lax.axis_index("client"), lax.axis_index("region")
    z, core = lax.div(region, 2), lax.rem(region, 2)
    clients = SIDE * SIDE
    plane = [{"client": lax.rem(client + d, clients)} for d in range(1, clients)]
    other = {"region": z * 2 + 1 - core}
    column = [{"region": lax.rem(z + d, depth) * 2 + core} for d in range(1, depth)]
    peers = plane + column + [other]
    barrier = pltpu.get_barrier_semaphore()
    for peer in peers:
        pl.semaphore_signal(barrier, inc=1, device_id=peer, device_id_type=MESH)

    tri = PlaneSum(copies, client, plane, tri_src, 0, tri_src.shape[0] // clients, tri_inbox)
    rest = PlaneSum(copies, client, plane, rest_src, 0, rest_src.shape[0] // clients, rest_inbox)

    def tri_done():
        pl.semaphore_wait(barrier, len(peers))
        start(tri.scatter)

    client_part(
        x_ref, r_ref, g_ref, t_ref, private_prior, tri_src, rest_src, corner_ref, z_ref, a_ref, leaf_ref, tri_done
    )
    arrive(tri.scatter)
    gather = tri.gather(tri_ref)
    tri.out[...] = tri.value()
    start(gather)
    arrive(gather)

    start(rest.scatter)
    rest_gather = rest.gather(rest_ref)
    region_block(tri_ref, regional_prior, a_ref)

    def halfway():
        arrive(rest.scatter)
        rest.out[...] = rest.value()
        start(rest_gather)

    invert(a_ref, leaf_ref, halfway)
    arrive(rest_gather)
    region_term(client, rest_ref, corner_ref, zr_ref, term_ref, a_ref, b_ref)

    rows = term_ref.shape[0] // 2
    base = pl.multiple_of(core * rows, 8)
    swapped = [copies.make(rows_of(term_ref, (1 - core) * rows, rows), swap, other)]
    start(swapped)
    arrive(swapped)
    pair[...] = term_ref[pl.ds(base, rows), :] + swap[...]
    term = PlaneSum(copies, client, plane, pair, 0, rows // clients, term_inbox)
    start(term.scatter)
    arrive(term.scatter)
    value = term.value()
    tiles = rows // clients // 8
    for t in range(tiles):
        tile[t] = value[8 * t : 8 * t + 8]
    across = [
        copies.make(tile.at[lax.rem(z + d + 1, tiles)], inbox.at[d], peer)
        for d, peer in enumerate(column)
    ]
    start(across)
    width_r = zr_ref.shape[0]
    z_ref[:, width_r:] = z_ref[:, width_r:] - mm3(z_ref[:, :width_r], zr_ref[...])
    arrive(across)
    me = lax.rem(z, tiles)
    final[me] = tree([tile[me]] + [inbox[d] for d in range(depth - 1)])
    near = []
    for d in range(1, tiles):
        peer = {"region": (z - me + lax.rem(me + d, tiles)) * 2 + core}
        near.append(copies.make(final.at[me], final.at[me], peer))
    start(near)
    arrive(near)
    term.at = base + client * term.rows
    gather = term.gather(total_ref)
    term.out[...] = jnp.concatenate([final[t] for t in range(tiles)], axis=0)
    start(gather)
    arrive(gather)
    mine = rows_of(total_ref, base, rows)
    swapped = [copies.make(mine, mine, other)]
    start(swapped)
    arrive(swapped)

    back_part(
        client, region, total_ref, global_prior, zr_ref, z_ref, private_ref, reg_ref, glob_ref, h_ref, full_ref, leaf_ref
    )
    copies.finish()


def solve(x, r, g, t, private_prior, regional_prior, global_prior, regions):
    p, width_r, width_g, rhs = x.shape[1], r.shape[1], g.shape[1], t.shape[1]
    depth, clients = regions // 2, SIDE * SIDE
    blocks = width_r // LEAF
    rest = width_g + rhs
    tri_rows = blocks * (blocks + 1) // 2 * LEAF
    rest_rows = width_r * rest // LEAF
    term_rows = width_g * rest // LEAF
    tiles = term_rows // 2 // clients // 8
    shapes = [
        (max(p, width_r), max(p, width_r)),
        (LEAF, LEAF),
        (p, width_r + rest),
        (tri_rows, LEAF),
        (rest_rows, LEAF),
        (width_g, rest),
        (tri_rows, LEAF),
        (rest_rows, LEAF),
        (width_r, rest),
        (width_r, rest),
        (term_rows, LEAF),
        (term_rows, LEAF),
        (width_g, width_g),
        (width_g, rhs),
        (term_rows // 2, LEAF),
        (term_rows // 2, LEAF),
        (depth - 1, 8, LEAF),
        (tiles, 8, LEAF),
        (tiles, 8, LEAF),
    ]
    for rows in (tri_rows, rest_rows, term_rows // 2):
        shapes.append((clients - 1, rows // clients, LEAF))
    sems = 256
    outs = [(p, rhs), (width_r // clients, rhs), (width_g // regions, rhs)]
    return pl.pallas_call(
        functools.partial(solve_kernel, depth),
        out_shape=[jax.ShapeDtypeStruct(s, F32) for s in outs],
        in_specs=[VMEM] * 7,
        out_specs=[VMEM] * len(outs),
        scratch_shapes=[pltpu.VMEM(s, F32) for s in shapes]
        + [pltpu.SemaphoreType.DMA((sems,)), pltpu.SemaphoreType.DMA((sems,))],
        compiler_params=pltpu.CompilerParams(collective_id=0, has_side_effects=True),
        name="solve",
    )(x, r, g, t, private_prior, regional_prior, global_prior)


def solution(mesh):
    regions = mesh.shape["region"]

    def per_device(x, r, g, t, private_prior, regional_prior, global_prior):
        private, regional, glob = solve(
            x[0, 0], r[0, 0], g[0, 0], t[0, 0], private_prior[0], regional_prior, global_prior[None], regions
        )
        return private[None, None], regional[None], glob

    placed = (
        P("region", "client", None, None),
        P("region", "client", None, None),
        P("region", "client", None, None),
        P("region", "client", None, None),
        P("region", "client", None),
        P("region", None),
        P(),
    )
    return jax.shard_map(
        per_device,
        mesh=mesh,
        in_specs=placed,
        out_specs=(
            P("region", "client", None, None),
            P("region", "client", None),
            P("region", None),
        ),
        check_vma=False,
    )
```

```python
import functools

import jax
import jax.numpy as jnp
from jax import lax
from jax.experimental import pallas as pl
from jax.experimental.pallas import tpu as pltpu
from jax.sharding import PartitionSpec as P

F32 = jnp.float32
BF16 = jnp.bfloat16
MESH = pl.DeviceIdType.MESH
HIGHEST = lax.Precision.HIGHEST
LEAF = 128
SIDE = 4
VMEM = pl.BlockSpec(memory_space=pltpu.VMEM)


def split(x):
    high = x.astype(BF16)
    return high, (x - high.astype(F32)).astype(BF16)


def mm(a, b):
    return jnp.dot(a, b, preferred_element_type=F32)


def mm3(a, b):
    a_high, a_low = split(a)
    b_high, b_low = split(b)
    return mm(
        jnp.concatenate([a_high, a_high, a_low], axis=1),
        jnp.concatenate([b_high, b_low, b_high], axis=0),
    )


def mm2(a, b):
    b_high, b_low = split(b)
    return mm(jnp.concatenate([a, a], axis=1), jnp.concatenate([b_high, b_low], axis=0))


def mm_full(a, b):
    return jnp.dot(a, b, preferred_element_type=F32, precision=HIGHEST)


def tree(terms):
    while len(terms) > 1:
        terms = [
            terms[i] + terms[i + 1] if i + 1 < len(terms) else terms[i]
            for i in range(0, len(terms), 2)
        ]
    return terms[0]


def leaf_inverse(m_ref):
    n = LEAF
    strips = n // 8
    lane = lax.broadcasted_iota(jnp.int32, (8, n), 1)
    sub = lax.broadcasted_iota(jnp.int32, (8, n), 0)
    is_row = [sub == k for k in range(8)]

    def row(v, k):
        return jnp.broadcast_to(v[k : k + 1, :], (8, n))

    def column(v, l):
        return jnp.broadcast_to(v[:, l : l + 1], (8, n))

    strip = [m_ref[8 * i : 8 * i + 8, :] for i in range(strips)]
    blank = jnp.zeros((8, n), F32)
    for k in range(strips):
        first = 8 * k
        cols = [column(strip[k], first + c) for c in range(8)]
        inside = (lane >= first) & (lane < first + 8)
        out = jnp.where(inside, jnp.where(lane - first == sub, 1.0, 0.0), strip[k])
        pivot = row(cols[0], 0)
        for p in range(8):
            r = pltpu.reciprocal(pivot, approx=True)
            if p < 7:
                ahead = row(cols[p + 1], p)
                pivot = row(cols[p + 1], p + 1) - (row(cols[p], p + 1) * ahead) * r
            for j in range(p + 1, 8):
                u = (ahead if j == p + 1 else row(cols[j], p)) * r
                cols[j] = jnp.where(is_row[p], u, cols[j] - cols[p] * u)
            u = row(out, p) * r
            out = jnp.where(is_row[p], u, out - cols[p] * u)
        after = strip[k + 1] if k + 1 < strips else None
        if after is not None:
            terms = [column(after, first + c) * row(out, c) for c in range(8)]
            after = jnp.where(inside, 0.0, after) - tree(terms)
        far = [i for i in range(strips) if i not in (k, k + 1)]
        product = mm3(
            jnp.concatenate([strip[i] for i in far], axis=0),
            jnp.concatenate([out if i == k else blank for i in range(strips)], axis=0),
        )
        for at, i in enumerate(far):
            strip[i] = jnp.where(inside, 0.0, strip[i]) - product[8 * at : 8 * at + 8]
        strip[k] = out
        if after is not None:
            strip[k + 1] = after
    for i in range(strips):
        m_ref[8 * i : 8 * i + 8, :] = strip[i]


def invert(a_ref, leaf_ref, opening=None, halfway=None):
    n = a_ref.shape[0]
    steps = n // LEAF

    @pl.loop(0, steps)
    def _(k):
        if halfway is not None:
            pl.when(k == steps // 2)(halfway)
        leaf_inverse(leaf_ref)
        if opening is not None:
            pl.when(k == 0)(opening)
        here = pl.ds(pl.multiple_of(k * LEAF, LEAF), LEAF)
        inverse = leaf_ref[...]
        down = a_ref[:, here]
        a_ref[here, :] = mm3(inverse, a_ref[here, :])
        a_ref[here, here] = inverse
        across = a_ref[here, :]
        a_ref[:, here] = jnp.zeros((n, LEAF), F32)
        a_ref[...] = a_ref[...] - mm3(down, across)
        a_ref[here, :] = across
        following = pl.ds(pl.multiple_of(lax.rem(k + 1, steps) * LEAF, LEAF), LEAF)
        leaf_ref[...] = a_ref[following, following]


def add_diagonal(x, diagonal):
    rows = lax.broadcasted_iota(jnp.int32, x.shape, 0)
    columns = lax.broadcasted_iota(jnp.int32, x.shape, 1)
    return x + jnp.where(rows == columns, diagonal, 0.0)


def client_part(x_ref, r_ref, g_ref, t_ref, prior_ref, tri_ref, rest_ref, corner_ref, z_ref, a_ref, leaf_ref, tri_done):
    x = x_ref[...]
    x_t = x.T
    a_ref[...] = add_diagonal(mm(x_t, x), prior_ref[...])
    leaf_ref[...] = a_ref[:LEAF, :LEAF]
    invert(a_ref, leaf_ref)
    a_high, a_low = split(a_ref[...])
    a_three = jnp.concatenate([a_high, a_high, a_low], axis=1)
    x_two = jnp.concatenate([x, x], axis=1)
    width_r = r_ref.shape[1]
    r_t, g_t = r_ref[...].T, g_ref[...].T
    step = 256

    def reduced(data, at):
        c_high, c_low = split(mm(x_t, data))
        z = mm(a_three, jnp.concatenate([c_high, c_low, c_high], axis=0))
        z_ref[:, at : at + step] = z
        return data.astype(F32) - mm(x_two, jnp.concatenate(split(z), axis=0))

    slot = 0
    for at in range(0, width_r, step):
        block = mm2(r_t[: at + step], reduced(r_ref[:, at : at + step], at))
        for j in range(at // LEAF, (at + step) // LEAF):
            lo = j * LEAF - at
            tri_ref[slot * LEAF : (slot + j + 1) * LEAF, :] = block[: (j + 1) * LEAF, lo : lo + LEAF]
            slot += j + 1
    tri_done()
    done = width_r
    for data_ref in (g_ref, t_ref):
        for at in range(0, data_ref.shape[1], step):
            residual = reduced(data_ref[:, at : at + step], done)
            block = mm2(r_t, residual)
            for lo in range(0, step, LEAF):
                row = (done - width_r + lo) // LEAF * width_r
                rest_ref[row : row + width_r, :] = block[:, lo : lo + LEAF]
            corner_ref[:, done - width_r : done - width_r + step] = mm2(g_t, residual)
            done += step


def region_block(tri_ref, prior_ref, a_ref):
    slot = 0
    for j in range(a_ref.shape[0] // LEAF):
        for i in range(j + 1):
            block = tri_ref[slot * LEAF : (slot + 1) * LEAF, :]
            a_ref[i * LEAF : (i + 1) * LEAF, j * LEAF : (j + 1) * LEAF] = block
            if i < j:
                a_ref[j * LEAF : (j + 1) * LEAF, i * LEAF : (i + 1) * LEAF] = block.T
            slot += 1
    a_ref[...] = add_diagonal(a_ref[...], prior_ref[...])


def region_term(client, rest_ref, corner_ref, zr_ref, term_ref, a_ref, b_ref):
    n = a_ref.shape[0]
    total = zr_ref.shape[1]
    for j in range(total // LEAF):
        b_ref[:, j * LEAF : (j + 1) * LEAF] = rest_ref[j * n : (j + 1) * n, :]
    zr_ref[...] = mm3(a_ref[...], b_ref[...])
    width_g = corner_ref.shape[0]
    share = n // (SIDE * SIDE)
    mine = pl.ds(pl.multiple_of(client * share, share), share)
    term = corner_ref[...] - mm_full(b_ref[mine, :width_g].T, zr_ref[mine, :])
    for j in range(total // LEAF):
        term_ref[j * width_g : (j + 1) * width_g, :] = term[:, j * LEAF : (j + 1) * LEAF]


def back_part(client, region, total_ref, prior_ref, zr_ref, z_ref, private_ref, reg_ref, glob_ref, h_ref, full_ref, leaf_ref):
    width_g = h_ref.shape[0]
    blocks = width_g // LEAF

    def block(j):
        return total_ref[j * width_g : (j + 1) * width_g, :]

    h_ref[...] = add_diagonal(
        jnp.concatenate([block(j) for j in range(blocks)], axis=1), prior_ref[...]
    )
    leaf_ref[...] = h_ref[:LEAF, :LEAF]
    invert(h_ref, leaf_ref)
    rhs = jnp.concatenate(
        [block(j) for j in range(blocks, total_ref.shape[0] // width_g)], axis=1
    )
    glob = mm3(h_ref[...], rhs)
    full_ref[...] = glob
    width_r = zr_ref.shape[0]
    ahead = z_ref.at[:, width_r:]
    private_ref[...] = ahead[:, width_g:] - mm3(ahead[:, :width_g], glob)
    share = reg_ref.shape[0]
    mine = pl.ds(pl.multiple_of(client * share, share), share)
    reg_ref[...] = zr_ref[mine, width_g:] - mm3(zr_ref[mine, :width_g], glob)
    share = glob_ref.shape[0]
    glob_ref[...] = full_ref[pl.ds(pl.multiple_of(region * share, share), share), :]


class Copies:
    def __init__(self, send_sem, recv_sem):
        self.send_sem, self.recv_sem, self.made = send_sem, recv_sem, []

    def make(self, src, dst, peer):
        used = len(self.made)
        copy = pltpu.make_async_remote_copy(
            src_ref=src,
            dst_ref=dst,
            send_sem=self.send_sem.at[used],
            recv_sem=self.recv_sem.at[used],
            device_id=peer,
            device_id_type=MESH,
        )
        self.made.append(copy)
        return copy

    def finish(self):
        for copy in self.made:
            copy.wait_send()


def start(copies):
    for copy in copies:
        copy.start()


def arrive(copies):
    for copy in copies:
        copy.wait_recv()


def rows_of(ref, at, rows):
    return ref.at[pl.ds(pl.multiple_of(at, 8), rows), :]


class PlaneSum:
    def __init__(self, copies, client, peers, src, base, rows, inbox):
        self.copies, self.inbox, self.rows, self.peers = copies, inbox, rows, peers
        self.own = rows_of(src, base + client * rows, rows)
        self.at = base + client * rows
        self.scatter = [
            copies.make(rows_of(src, base + peer["client"] * rows, rows), inbox.at[d], peer)
            for d, peer in enumerate(peers)
        ]

    def value(self):
        return tree([self.own[...]] + [self.inbox[d] for d in range(len(self.peers))])

    def gather(self, out):
        self.out = rows_of(out, self.at, self.rows)
        return [self.copies.make(self.out, self.out, peer) for peer in self.peers]


def solve_kernel(
    depth,
    x_ref,
    r_ref,
    g_ref,
    t_ref,
    private_prior,
    regional_prior,
    global_prior,
    private_ref,
    reg_ref,
    glob_ref,
    a_ref,
    leaf_ref,
    z_ref,
    tri_src,
    rest_src,
    corner_ref,
    tri_ref,
    rest_ref,
    b_ref,
    zr_ref,
    term_ref,
    total_ref,
    h_ref,
    full_ref,
    swap,
    pair,
    inbox,
    tile,
    final,
    corner_inbox,
    tri_inbox,
    rest_inbox,
    term_inbox,
    send_sem,
    recv_sem,
):
    copies = Copies(send_sem, recv_sem)
    client, region = lax.axis_index("client"), lax.axis_index("region")
    z, core = lax.div(region, 2), lax.rem(region, 2)
    clients = SIDE * SIDE
    plane = [{"client": lax.rem(client + d, clients)} for d in range(1, clients)]
    other = {"region": z * 2 + 1 - core}
    column = [{"region": lax.rem(z + d, depth) * 2 + core} for d in range(1, depth)]
    peers = plane + column + [other]
    barrier = pltpu.get_barrier_semaphore()
    for peer in peers:
        pl.semaphore_signal(barrier, inc=1, device_id=peer, device_id_type=MESH)

    corner = PlaneSum(copies, client, plane, tri_src, 0, LEAF // clients, corner_inbox)
    tri_rows = (tri_src.shape[0] - LEAF) // clients
    tri = PlaneSum(copies, client, plane, tri_src, LEAF, tri_rows, tri_inbox)
    rest = PlaneSum(copies, client, plane, rest_src, 0, rest_src.shape[0] // clients, rest_inbox)
    corner_gather = corner.gather(tri_ref)
    tri_gather = tri.gather(tri_ref)
    rest_gather = rest.gather(rest_ref)

    def tri_done():
        pl.semaphore_wait(barrier, len(peers))
        start(corner.scatter)
        start(tri.scatter)

    client_part(
        x_ref, r_ref, g_ref, t_ref, private_prior, tri_src, rest_src, corner_ref, z_ref, a_ref, leaf_ref, tri_done
    )
    arrive(corner.scatter)
    corner.out[...] = corner.value()
    start(corner_gather)
    arrive(tri.scatter)
    tri.out[...] = tri.value()
    start(tri_gather)
    start(rest.scatter)
    arrive(corner_gather)
    leaf_ref[...] = add_diagonal(tri_ref[:LEAF, :], regional_prior[:, :LEAF])

    def opening():
        arrive(tri_gather)
        region_block(tri_ref, regional_prior, a_ref)

    def halfway():
        arrive(rest.scatter)
        rest.out[...] = rest.value()
        start(rest_gather)

    invert(a_ref, leaf_ref, opening, halfway)
    arrive(rest_gather)
    region_term(client, rest_ref, corner_ref, zr_ref, term_ref, a_ref, b_ref)

    rows = term_ref.shape[0] // 2
    base = pl.multiple_of(core * rows, 8)
    swapped = [copies.make(rows_of(term_ref, (1 - core) * rows, rows), swap, other)]
    start(swapped)
    arrive(swapped)
    pair[...] = term_ref[pl.ds(base, rows), :] + swap[...]
    term = PlaneSum(copies, client, plane, pair, 0, rows // clients, term_inbox)
    start(term.scatter)
    arrive(term.scatter)
    value = term.value()
    tiles = rows // clients // 8
    for t in range(tiles):
        tile[t] = value[8 * t : 8 * t + 8]
    across = [
        copies.make(tile.at[lax.rem(z + d + 1, tiles)], inbox.at[d], peer)
        for d, peer in enumerate(column)
    ]
    start(across)
    width_r = zr_ref.shape[0]
    z_ref[:, width_r:] = z_ref[:, width_r:] - mm3(z_ref[:, :width_r], zr_ref[...])
    arrive(across)
    me = lax.rem(z, tiles)
    final[me] = tree([tile[me]] + [inbox[d] for d in range(depth - 1)])
    near = []
    for d in range(1, tiles):
        peer = {"region": (z - me + lax.rem(me + d, tiles)) * 2 + core}
        near.append(copies.make(final.at[me], final.at[me], peer))
    start(near)
    arrive(near)
    term.at = base + client * term.rows
    gather = term.gather(total_ref)
    term.out[...] = jnp.concatenate([final[t] for t in range(tiles)], axis=0)
    start(gather)
    arrive(gather)
    mine = rows_of(total_ref, base, rows)
    swapped = [copies.make(mine, mine, other)]
    start(swapped)
    arrive(swapped)

    back_part(
        client, region, total_ref, global_prior, zr_ref, z_ref, private_ref, reg_ref, glob_ref, h_ref, full_ref, leaf_ref
    )
    copies.finish()


def finish_kernel(*refs):
    count = len(refs) // 2
    for source, out in zip(refs[:count], refs[count:]):
        out[...] = source[...]


def finish(*arrays):
    return pl.pallas_call(
        finish_kernel,
        out_shape=[jax.ShapeDtypeStruct(a.shape, F32) for a in arrays],
        in_specs=[VMEM] * len(arrays),
        out_specs=[VMEM] * len(arrays),
        name="finish",
    )(*arrays)


def solve(x, r, g, t, private_prior, regional_prior, global_prior, regions):
    p, width_r, width_g, rhs = x.shape[1], r.shape[1], g.shape[1], t.shape[1]
    depth, clients = regions // 2, SIDE * SIDE
    blocks = width_r // LEAF
    rest = width_g + rhs
    tri_rows = blocks * (blocks + 1) // 2 * LEAF
    rest_rows = width_r * rest // LEAF
    term_rows = width_g * rest // LEAF
    tiles = term_rows // 2 // clients // 8
    shapes = [
        (max(p, width_r), max(p, width_r)),
        (LEAF, LEAF),
        (p, width_r + rest),
        (tri_rows, LEAF),
        (rest_rows, LEAF),
        (width_g, rest),
        (tri_rows, LEAF),
        (rest_rows, LEAF),
        (width_r, rest),
        (width_r, rest),
        (term_rows, LEAF),
        (term_rows, LEAF),
        (width_g, width_g),
        (width_g, rhs),
        (term_rows // 2, LEAF),
        (term_rows // 2, LEAF),
        (depth - 1, 8, LEAF),
        (tiles, 8, LEAF),
        (tiles, 8, LEAF),
    ]
    for rows in (LEAF, tri_rows - LEAF, rest_rows, term_rows // 2):
        shapes.append((clients - 1, rows // clients, LEAF))
    sems = 256
    outs = [(p, rhs), (width_r // clients, rhs), (width_g // regions, rhs)]
    return pl.pallas_call(
        functools.partial(solve_kernel, depth),
        out_shape=[jax.ShapeDtypeStruct(s, F32) for s in outs],
        in_specs=[VMEM] * 7,
        out_specs=[VMEM] * len(outs),
        scratch_shapes=[pltpu.VMEM(s, F32) for s in shapes]
        + [pltpu.SemaphoreType.DMA((sems,)), pltpu.SemaphoreType.DMA((sems,))],
        compiler_params=pltpu.CompilerParams(collective_id=0, has_side_effects=True),
        name="solve",
    )(x, r, g, t, private_prior, regional_prior, global_prior)


def solution(mesh):
    regions = mesh.shape["region"]

    def per_device(x, r, g, t, private_prior, regional_prior, global_prior):
        private, regional, glob = solve(
            x[0, 0], r[0, 0], g[0, 0], t[0, 0], private_prior[0], regional_prior, global_prior[None], regions
        )
        private, regional, glob = finish(private, regional, glob)
        return private[None, None], regional[None], glob

    placed = (
        P("region", "client", None, None),
        P("region", "client", None, None),
        P("region", "client", None, None),
        P("region", "client", None, None),
        P("region", "client", None),
        P("region", None),
        P(),
    )
    return jax.shard_map(
        per_device,
        mesh=mesh,
        in_specs=placed,
        out_specs=(
            P("region", "client", None, None),
            P("region", "client", None),
            P("region", None),
        ),
        check_vma=False,
    )
```

```python
import functools

import jax
import jax.numpy as jnp
from jax import lax
from jax.experimental import pallas as pl
from jax.experimental.pallas import tpu as pltpu
from jax.sharding import PartitionSpec as P

F32 = jnp.float32
BF16 = jnp.bfloat16
MESH = pl.DeviceIdType.MESH
LEAF = 128
SIDE = 4
VMEM = pl.BlockSpec(memory_space=pltpu.VMEM)


def split(x):
    high = x.astype(BF16)
    return high, (x - high.astype(F32)).astype(BF16)


def mm(a, b):
    return jnp.dot(a, b, preferred_element_type=F32)


def mm3(a, b):
    a_high, a_low = split(a)
    b_high, b_low = split(b)
    return mm(
        jnp.concatenate([a_high, a_high, a_low], axis=1),
        jnp.concatenate([b_high, b_low, b_high], axis=0),
    )


def mm2(a, b):
    b_high, b_low = split(b)
    return mm(jnp.concatenate([a, a], axis=1), jnp.concatenate([b_high, b_low], axis=0))


def tree(terms):
    while len(terms) > 1:
        terms = [
            terms[i] + terms[i + 1] if i + 1 < len(terms) else terms[i]
            for i in range(0, len(terms), 2)
        ]
    return terms[0]


def leaf_inverse(m_ref):
    n = LEAF
    strips = n // 8
    lane = lax.broadcasted_iota(jnp.int32, (8, n), 1)
    sub = lax.broadcasted_iota(jnp.int32, (8, n), 0)
    is_row = [sub == k for k in range(8)]

    def row(v, k):
        return jnp.broadcast_to(v[k : k + 1, :], (8, n))

    def column(v, l):
        return jnp.broadcast_to(v[:, l : l + 1], (8, n))

    strip = [m_ref[8 * i : 8 * i + 8, :] for i in range(strips)]
    blank = jnp.zeros((8, n), F32)
    for k in range(strips):
        first = 8 * k
        cols = [column(strip[k], first + c) for c in range(8)]
        inside = (lane >= first) & (lane < first + 8)
        out = jnp.where(inside, jnp.where(lane - first == sub, 1.0, 0.0), strip[k])
        pivot = row(cols[0], 0)
        for p in range(8):
            r = pltpu.reciprocal(pivot, approx=True)
            if p < 7:
                ahead = row(cols[p + 1], p)
                pivot = row(cols[p + 1], p + 1) - (row(cols[p], p + 1) * ahead) * r
            for j in range(p + 1, 8):
                u = (ahead if j == p + 1 else row(cols[j], p)) * r
                cols[j] = jnp.where(is_row[p], u, cols[j] - cols[p] * u)
            u = row(out, p) * r
            out = jnp.where(is_row[p], u, out - cols[p] * u)
        after = strip[k + 1] if k + 1 < strips else None
        if after is not None:
            terms = [column(after, first + c) * row(out, c) for c in range(8)]
            after = jnp.where(inside, 0.0, after) - tree(terms)
        far = [i for i in range(strips) if i not in (k, k + 1)]
        product = mm3(
            jnp.concatenate([strip[i] for i in far], axis=0),
            jnp.concatenate([out if i == k else blank for i in range(strips)], axis=0),
        )
        for at, i in enumerate(far):
            strip[i] = jnp.where(inside, 0.0, strip[i]) - product[8 * at : 8 * at + 8]
        strip[k] = out
        if after is not None:
            strip[k + 1] = after
    for i in range(strips):
        m_ref[8 * i : 8 * i + 8, :] = strip[i]


def invert(a_ref, leaf_ref, opening=None, halfway=None):
    n = a_ref.shape[0]
    steps = n // LEAF

    @pl.loop(0, steps)
    def _(k):
        if halfway is not None:
            pl.when(k == steps // 2)(halfway)
        leaf_inverse(leaf_ref)
        if opening is not None:
            pl.when(k == 0)(opening)
        here = pl.ds(pl.multiple_of(k * LEAF, LEAF), LEAF)
        inverse = leaf_ref[...]
        down = a_ref[:, here]
        a_ref[here, :] = mm3(inverse, a_ref[here, :])
        a_ref[here, here] = inverse
        across = a_ref[here, :]
        a_ref[:, here] = jnp.zeros((n, LEAF), F32)
        a_ref[...] = a_ref[...] - mm3(down, across)
        a_ref[here, :] = across
        following = pl.ds(pl.multiple_of(lax.rem(k + 1, steps) * LEAF, LEAF), LEAF)
        leaf_ref[...] = a_ref[following, following]


def add_diagonal(x, diagonal):
    rows = lax.broadcasted_iota(jnp.int32, x.shape, 0)
    columns = lax.broadcasted_iota(jnp.int32, x.shape, 1)
    return x + jnp.where(rows == columns, diagonal, 0.0)


def client_part(x_ref, r_ref, g_ref, t_ref, prior_ref, tri_ref, rest_ref, corner_ref, z_ref, a_ref, leaf_ref, chunk_done):
    x = x_ref[...]
    x_t = x.T
    a_ref[...] = add_diagonal(mm(x_t, x), prior_ref[...])
    leaf_ref[...] = a_ref[:LEAF, :LEAF]
    invert(a_ref, leaf_ref)
    a_high, a_low = split(a_ref[...])
    a_three = jnp.concatenate([a_high, a_high, a_low], axis=1)
    x_two = jnp.concatenate([x, x], axis=1)
    width_r = r_ref.shape[1]
    r_t, g_t = r_ref[...].T, g_ref[...].T
    step = 256

    def reduced(data, at):
        c_high, c_low = split(mm(x_t, data))
        z = mm(a_three, jnp.concatenate([c_high, c_low, c_high], axis=0))
        z_ref[:, at : at + step] = z
        return data.astype(F32) - mm(x_two, jnp.concatenate(split(z), axis=0))

    slot = 0
    for at in range(0, width_r, step):
        block = mm2(r_t[: at + step], reduced(r_ref[:, at : at + step], at))
        for j in range(at // LEAF, (at + step) // LEAF):
            lo = j * LEAF - at
            tri_ref[slot * LEAF : (slot + j + 1) * LEAF, :] = block[: (j + 1) * LEAF, lo : lo + LEAF]
            slot += j + 1
        chunk_done(at // step)
    done = width_r
    for data_ref in (g_ref, t_ref):
        for at in range(0, data_ref.shape[1], step):
            residual = reduced(data_ref[:, at : at + step], done)
            block = mm2(r_t, residual)
            for lo in range(0, step, LEAF):
                row = (done - width_r + lo) // LEAF * width_r
                rest_ref[row : row + width_r, :] = block[:, lo : lo + LEAF]
            corner_ref[:, done - width_r : done - width_r + step] = mm2(g_t, residual)
            done += step


def region_block(tri_ref, prior_ref, a_ref):
    slot = 0
    for j in range(a_ref.shape[0] // LEAF):
        for i in range(j + 1):
            block = tri_ref[slot * LEAF : (slot + 1) * LEAF, :]
            a_ref[i * LEAF : (i + 1) * LEAF, j * LEAF : (j + 1) * LEAF] = block
            if i < j:
                a_ref[j * LEAF : (j + 1) * LEAF, i * LEAF : (i + 1) * LEAF] = block.T
            slot += 1
    a_ref[...] = add_diagonal(a_ref[...], prior_ref[...])


def region_term(client, rest_ref, corner_ref, zr_ref, term_ref, a_ref, b_ref):
    n = a_ref.shape[0]
    total = zr_ref.shape[1]
    for j in range(total // LEAF):
        b_ref[:, j * LEAF : (j + 1) * LEAF] = rest_ref[j * n : (j + 1) * n, :]
    width_g = corner_ref.shape[0]
    share = n // (SIDE * SIDE)
    mine = pl.ds(pl.multiple_of(client * share, share), share)
    term = corner_ref[...] - mm3(b_ref[mine, :width_g].T, mm3(a_ref[mine, :], b_ref[...]))
    for j in range(total // LEAF):
        term_ref[j * width_g : (j + 1) * width_g, :] = term[:, j * LEAF : (j + 1) * LEAF]


def back_part(client, region, total_ref, prior_ref, zr_ref, z_ref, private_ref, reg_ref, glob_ref, h_ref, full_ref, leaf_ref):
    width_g = h_ref.shape[0]
    blocks = width_g // LEAF

    def block(j):
        return total_ref[j * width_g : (j + 1) * width_g, :]

    h_ref[...] = add_diagonal(
        jnp.concatenate([block(j) for j in range(blocks)], axis=1), prior_ref[...]
    )
    leaf_ref[...] = h_ref[:LEAF, :LEAF]
    invert(h_ref, leaf_ref)
    rhs = jnp.concatenate(
        [block(j) for j in range(blocks, total_ref.shape[0] // width_g)], axis=1
    )
    glob = mm3(h_ref[...], rhs)
    full_ref[...] = glob
    width_r = zr_ref.shape[0]
    ahead = z_ref.at[:, width_r:]
    private_ref[...] = ahead[:, width_g:] - mm3(ahead[:, :width_g], glob)
    share = reg_ref.shape[0]
    mine = pl.ds(pl.multiple_of(client * share, share), share)
    reg_ref[...] = zr_ref[mine, width_g:] - mm3(zr_ref[mine, :width_g], glob)
    share = glob_ref.shape[0]
    glob_ref[...] = full_ref[pl.ds(pl.multiple_of(region * share, share), share), :]


class Copies:
    def __init__(self, send_sem, recv_sem):
        self.send_sem, self.recv_sem, self.made = send_sem, recv_sem, []

    def make(self, src, dst, peer):
        used = len(self.made)
        copy = pltpu.make_async_remote_copy(
            src_ref=src,
            dst_ref=dst,
            send_sem=self.send_sem.at[used],
            recv_sem=self.recv_sem.at[used],
            device_id=peer,
            device_id_type=MESH,
        )
        self.made.append(copy)
        return copy

    def finish(self):
        for copy in self.made:
            copy.wait_send()


def start(copies):
    for copy in copies:
        copy.start()


def arrive(copies):
    for copy in copies:
        copy.wait_recv()


def rows_of(ref, at, rows):
    return ref.at[pl.ds(pl.multiple_of(at, 8), rows), :]


class PlaneSum:
    def __init__(self, copies, client, peers, src, base, rows, inbox):
        self.copies, self.inbox, self.rows, self.peers = copies, inbox, rows, peers
        self.own = rows_of(src, base + client * rows, rows)
        self.at = base + client * rows
        self.scatter = [
            copies.make(rows_of(src, base + peer["client"] * rows, rows), inbox.at[d], peer)
            for d, peer in enumerate(peers)
        ]

    def value(self):
        return tree([self.own[...]] + [self.inbox[d] for d in range(len(self.peers))])

    def gather(self, out):
        self.out = rows_of(out, self.at, self.rows)
        return [self.copies.make(self.out, self.out, peer) for peer in self.peers]


def solve_kernel(
    depth,
    x_ref,
    r_ref,
    g_ref,
    t_ref,
    private_prior,
    regional_prior,
    global_prior,
    private_ref,
    reg_ref,
    glob_ref,
    a_ref,
    leaf_ref,
    z_ref,
    tri_src,
    rest_src,
    corner_ref,
    tri_ref,
    rest_ref,
    b_ref,
    zr_ref,
    term_ref,
    total_ref,
    h_ref,
    full_ref,
    swap,
    pair,
    inbox,
    tile,
    final,
    corner_inbox,
    early_inbox,
    late_inbox,
    rest_inbox,
    term_inbox,
    send_sem,
    recv_sem,
):
    copies = Copies(send_sem, recv_sem)
    client, region = lax.axis_index("client"), lax.axis_index("region")
    z, core = lax.div(region, 2), lax.rem(region, 2)
    clients = SIDE * SIDE
    plane = [{"client": lax.rem(client + d, clients)} for d in range(1, clients)]
    other = {"region": z * 2 + 1 - core}
    column = [{"region": lax.rem(z + d, depth) * 2 + core} for d in range(1, depth)]
    peers = plane + column + [other]
    barrier = pltpu.get_barrier_semaphore()
    for peer in peers:
        pl.semaphore_signal(barrier, inc=1, device_id=peer, device_id_type=MESH)

    corner = PlaneSum(copies, client, plane, tri_src, 0, LEAF // clients, corner_inbox)
    early = PlaneSum(copies, client, plane, tri_src, LEAF, 2 * LEAF // clients, early_inbox)
    late_rows = (tri_src.shape[0] - 3 * LEAF) // clients
    late = PlaneSum(copies, client, plane, tri_src, 3 * LEAF, late_rows, late_inbox)
    rest = PlaneSum(copies, client, plane, rest_src, 0, rest_src.shape[0] // clients, rest_inbox)
    corner_gather = corner.gather(tri_ref)
    early_gather = early.gather(tri_ref)
    late_gather = late.gather(tri_ref)
    rest_gather = rest.gather(rest_ref)

    def chunk_done(chunk):
        if chunk == 0:
            pl.semaphore_wait(barrier, len(peers))
            start(corner.scatter)
            start(early.scatter)
        else:
            start(late.scatter)

    client_part(
        x_ref, r_ref, g_ref, t_ref, private_prior, tri_src, rest_src, corner_ref, z_ref, a_ref, leaf_ref, chunk_done
    )
    arrive(corner.scatter)
    corner.out[...] = corner.value()
    start(corner_gather)
    for part, gather in ((early, early_gather), (late, late_gather)):
        arrive(part.scatter)
        part.out[...] = part.value()
        start(gather)
    start(rest.scatter)
    arrive(corner_gather)
    leaf_ref[...] = add_diagonal(tri_ref[:LEAF, :], regional_prior[:, :LEAF])

    def opening():
        arrive(early_gather)
        arrive(late_gather)
        region_block(tri_ref, regional_prior, a_ref)

    def halfway():
        arrive(rest.scatter)
        rest.out[...] = rest.value()
        start(rest_gather)

    invert(a_ref, leaf_ref, opening, halfway)
    arrive(rest_gather)
    region_term(client, rest_ref, corner_ref, zr_ref, term_ref, a_ref, b_ref)

    rows = term_ref.shape[0] // 2
    base = pl.multiple_of(core * rows, 8)
    swapped = [copies.make(rows_of(term_ref, (1 - core) * rows, rows), swap, other)]
    start(swapped)
    arrive(swapped)
    pair[...] = term_ref[pl.ds(base, rows), :] + swap[...]
    term = PlaneSum(copies, client, plane, pair, 0, rows // clients, term_inbox)
    start(term.scatter)
    zr_ref[...] = mm3(a_ref[...], b_ref[...])
    arrive(term.scatter)
    value = term.value()
    tiles = rows // clients // 8
    for t in range(tiles):
        tile[t] = value[8 * t : 8 * t + 8]
    across = [
        copies.make(tile.at[lax.rem(z + d + 1, tiles)], inbox.at[d], peer)
        for d, peer in enumerate(column)
    ]
    start(across)
    width_r = zr_ref.shape[0]
    z_ref[:, width_r:] = z_ref[:, width_r:] - mm3(z_ref[:, :width_r], zr_ref[...])
    arrive(across)
    me = lax.rem(z, tiles)
    final[me] = tree([tile[me]] + [inbox[d] for d in range(depth - 1)])
    near = []
    for d in range(1, tiles):
        peer = {"region": (z - me + lax.rem(me + d, tiles)) * 2 + core}
        near.append(copies.make(final.at[me], final.at[me], peer))
    start(near)
    arrive(near)
    term.at = base + client * term.rows
    gather = term.gather(total_ref)
    term.out[...] = jnp.concatenate([final[t] for t in range(tiles)], axis=0)
    start(gather)
    arrive(gather)
    mine = rows_of(total_ref, base, rows)
    swapped = [copies.make(mine, mine, other)]
    start(swapped)
    arrive(swapped)

    back_part(
        client, region, total_ref, global_prior, zr_ref, z_ref, private_ref, reg_ref, glob_ref, h_ref, full_ref, leaf_ref
    )
    copies.finish()


def finish_kernel(*refs):
    count = len(refs) // 2
    for source, out in zip(refs[:count], refs[count:]):
        out[...] = source[...]


def finish(*arrays):
    return pl.pallas_call(
        finish_kernel,
        out_shape=[jax.ShapeDtypeStruct(a.shape, F32) for a in arrays],
        in_specs=[VMEM] * len(arrays),
        out_specs=[VMEM] * len(arrays),
        name="finish",
    )(*arrays)


def solve(x, r, g, t, private_prior, regional_prior, global_prior, regions):
    p, width_r, width_g, rhs = x.shape[1], r.shape[1], g.shape[1], t.shape[1]
    depth, clients = regions // 2, SIDE * SIDE
    blocks = width_r // LEAF
    rest = width_g + rhs
    tri_rows = blocks * (blocks + 1) // 2 * LEAF
    rest_rows = width_r * rest // LEAF
    term_rows = width_g * rest // LEAF
    tiles = term_rows // 2 // clients // 8
    shapes = [
        (max(p, width_r), max(p, width_r)),
        (LEAF, LEAF),
        (p, width_r + rest),
        (tri_rows, LEAF),
        (rest_rows, LEAF),
        (width_g, rest),
        (tri_rows, LEAF),
        (rest_rows, LEAF),
        (width_r, rest),
        (width_r, rest),
        (term_rows, LEAF),
        (term_rows, LEAF),
        (width_g, width_g),
        (width_g, rhs),
        (term_rows // 2, LEAF),
        (term_rows // 2, LEAF),
        (depth - 1, 8, LEAF),
        (tiles, 8, LEAF),
        (tiles, 8, LEAF),
    ]
    for rows in (LEAF, 2 * LEAF, tri_rows - 3 * LEAF, rest_rows, term_rows // 2):
        shapes.append((clients - 1, rows // clients, LEAF))
    sems = 256
    outs = [(p, rhs), (width_r // clients, rhs), (width_g // regions, rhs)]
    return pl.pallas_call(
        functools.partial(solve_kernel, depth),
        out_shape=[jax.ShapeDtypeStruct(s, F32) for s in outs],
        in_specs=[VMEM] * 7,
        out_specs=[VMEM] * len(outs),
        scratch_shapes=[pltpu.VMEM(s, F32) for s in shapes]
        + [pltpu.SemaphoreType.DMA((sems,)), pltpu.SemaphoreType.DMA((sems,))],
        compiler_params=pltpu.CompilerParams(collective_id=0, has_side_effects=True),
        name="solve",
    )(x, r, g, t, private_prior, regional_prior, global_prior)


def solution(mesh):
    regions = mesh.shape["region"]

    def per_device(x, r, g, t, private_prior, regional_prior, global_prior):
        private, regional, glob = solve(
            x[0, 0], r[0, 0], g[0, 0], t[0, 0], private_prior[0], regional_prior, global_prior[None], regions
        )
        private, regional, glob = finish(private, regional, glob)
        return private[None, None], regional[None], glob

    placed = (
        P("region", "client", None, None),
        P("region", "client", None, None),
        P("region", "client", None, None),
        P("region", "client", None, None),
        P("region", "client", None),
        P("region", None),
        P(),
    )
    return jax.shard_map(
        per_device,
        mesh=mesh,
        in_specs=placed,
        out_specs=(
            P("region", "client", None, None),
            P("region", "client", None),
            P("region", None),
        ),
        check_vma=False,
    )
```
